32 devices in a mesh: dp: 4 (over x, core), ctx: 8 (over z, y).
Axes of the slice: x: 2, y: 2, z: 4, core: 2. Of those that a mesh axis runs over, the one named last changes fastest.
Arguments:
- merged_grad: bfloat16 [4096, 1792], P(('dp', 'ctx')), may hold values from -6 to 6
- merged_owner: int32 [4096, 1], P(('dp', 'ctx')), may hold values from 0 to 7; in each aligned block of 128 rows (0 to 127, 128 to 255, ...) at most 32 rows name the same one
- merger_pre: bfloat16 [8192, 2560], P(('dp', 'ctx')), may hold values from -6 to 6
- fc2_weight: bfloat16 [2560, 1792], P('ctx'), may hold values from -0.125 to 0.125
- query: bfloat16 [8192, 1280], P(('dp', 'ctx')), may hold values from -32 to 32
- key_states: bfloat16 [8192, 1280], P(('dp', 'ctx')), may hold values from -32 to 32
- value_states: bfloat16 [8192, 1280], P(('dp', 'ctx')), may hold values from -6 to 6
- out_grad: bfloat16 [8192, 1280], P(('dp', 'ctx')), may hold values from -6 to 6
- position: int32 [2, 8192], P(None, ('dp', 'ctx')), may hold values from 0 to 63, as said below
Outputs:
- hidden_grad: bfloat16 [8192, 2560], P(('dp', 'ctx'))
- weight_grad: float32 [2560, 1792], P('ctx', 'dp')
- query_grad: bfloat16 [8192, 1280], P(('dp', 'ctx'))
- key_grad: bfloat16 [8192, 1280], P(('dp', 'ctx'))
- value_grad: bfloat16 [8192, 1280], P(('dp', 'ctx'))
The draws below stay inside these ranges and needn't reach their ends.
Inputs may be any that keep to these rules, and one draw needn't show every extreme that they name: `merged_owner`: in each device's block of 128 rows no owner is named more than 32 times. `position`: each window of 64 consecutive patches covers an aligned square of 8 by 8 grid positions, row by row.
All inputs are finite; a program needn't handle non-finite values.
Results may differ from the reference program's by a relative error of at most 0.0017.
The reference program's roundings to bfloat16 on the way (of `slotted`, `act`, `q_rot`, `k_rot`, `probs_b` and `score_grad`) count: a program that leaves them out, or rounds other values in their place, can miss the bound.
Values may be sent and summed in bfloat16 or wider, within the bound.
A program may use at most 128 MiB of HBM per device.

```python
import math
import jax
import jax.numpy as jnp
import numpy as np
from jax import lax

D = 1280
HEADS = 16
HEAD = 80
WIN_SIDE = 8
WIN = 64
HID = 2560
OUTW = 1792
G_DEV = 128
PATCH_DEV = 256
CAP = 32
SLOTS = 256
TOKENS = 4096
ALLSLOTS = 8192
PATCHES = 8192
N_DP = 4
N_CTX = 8


def window_positions(key):
    pkey = jax.random.fold_in(key, 7)
    windows = PATCHES // WIN
    corner = jax.random.randint(pkey, (2, windows), 0, WIN_SIDE, dtype=jnp.int32)
    inside = jnp.arange(WIN, dtype=jnp.int32)
    rows = corner[0][:, None] * WIN_SIDE + inside[None, :] // WIN_SIDE
    cols = corner[1][:, None] * WIN_SIDE + inside[None, :] % WIN_SIDE
    return jnp.stack([rows.reshape(-1), cols.reshape(-1)])


def drawn_pair(key):
    query = jax.random.normal(jax.random.fold_in(key, 11), (PATCHES, HEADS, HEAD), jnp.float32)
    keys = jax.random.normal(jax.random.fold_in(key, 12), (PATCHES, HEADS, HEAD), jnp.float32)
    return (query.reshape(PATCHES, D), keys.reshape(PATCHES, D))


def draw_query(key, part):
    return drawn_pair(key)[0].astype(jnp.bfloat16)


def draw_key_states(key, part):
    return drawn_pair(key)[1].astype(jnp.bfloat16)


def draw_position(key, part):
    return window_positions(key)


def with_spikes(entries, rng, source, target, parts, factor):
    def block_of(dim):
        return (jnp.arange(entries.shape[dim]) // (entries.shape[dim] // parts)).reshape((-1,) + (1,) * (entries.ndim - 1 - dim))

    first = jax.random.permutation(rng, parts)[block_of(target)]
    far = (block_of(target) + parts // 2) % parts
    return jnp.where((block_of(source) == first) | (block_of(source) == far), factor * entries, entries)


def block_scale(key, dims, split, low, top_value):
    gain, own = 1.0, jax.random.fold_in(key, 6)
    for dim, blocks in split:
        steps = jnp.exp(jax.random.uniform(jax.random.fold_in(own, dim), (blocks,), jnp.float32, low / len(split), top_value / len(split)))
        gain = gain * jnp.repeat(steps, dims[dim] // blocks).reshape([-1 if axis == dim else 1 for axis in range(len(dims))])
    return gain


def routed_block(key, own, number, rows, amount, top, reach, lean):
    sequence = jax.random.permutation(key, amount)
    heavy_load, usual = load_shares(amount, rows * top, reach, lean, True), load_shares(amount, rows * top, reach, lean, False)
    places = jnp.arange(amount)

    def named(tallies, turn):
        used = int((tallies > 0).sum())
        fixed = max(1, used // 4)
        moved = fixed + (places - fixed + turn * (used - fixed)) % max(1, amount - fixed)
        return jnp.zeros((amount,), jnp.int32).at[sequence[jnp.where(places < fixed, places, moved)]].set(jnp.asarray(tallies, jnp.int32))

    tallies = jnp.where(number % 4 == 0, named(heavy_load, number // 4), named(usual, number - number // 4 - 1))
    mixed = jax.random.permutation(jax.random.fold_in(own, 3), amount)
    source_of, sink = mixed[0:amount // 2 * 2:2], mixed[1:amount // 2 * 2:2]
    slack = jnp.minimum(tallies[source_of] - 1, reach - tallies[sink]) // 2
    slack = jnp.where((source_of == sequence[0]) | (sink == sequence[0]) | (tallies[sink] == 0), 0, jnp.maximum(slack, 0))
    moved = jax.random.randint(jax.random.fold_in(own, 4), (amount // 2,), 0, 1 << 20) % (slack + 1)
    tallies = tallies.at[source_of].add(-moved).at[sink].add(moved)
    members = jnp.searchsorted(jnp.cumsum(tallies), jnp.arange(rows * top), side="right").astype(jnp.int32)
    grid = members.reshape(top, rows).T
    grid = grid[jax.random.permutation(jax.random.fold_in(own, 1), rows)]
    turn = jax.random.randint(jax.random.fold_in(own, 2), (rows, 1), 0, top)
    return jnp.take_along_axis(grid, (jnp.arange(top)[None, :] + turn) % top, axis=1)


def load_shares(count, total, bound, skew, full):
    weights = [(1 << 20) // math.isqrt(standing ** skew) + 1 for standing in range(1, count + 1)]
    largest = bound if full else min(bound, max(-(-total // count), total * weights[0] // sum(weights)))
    least = 1 if total - largest >= count - 1 else 0
    given, spare = [largest] + [least] * (count - 1), total - largest - least * (count - 1)
    while spare > 0:
        movable = [i for i in range(1, count) if given[i] < largest] or [i for i in range(1, count) if given[i] < bound]
        pool, left = sum([weights[i] for i in movable]), spare
        for i in movable:
            extra = min(bound - given[i], max(1, left * weights[i] // pool), spare)
            given[i] = given[i] + extra
            spare = spare - extra
    return np.array(given)


def noise(stream_key, dims, deviation, limit, cuts=(), held_as=jnp.bfloat16):
    values = deviation * jax.random.normal(stream_key, dims, jnp.float32)
    if cuts:
        values = values * block_scale(stream_key, dims, cuts, -0.22, 0.18)
    return jnp.clip(values, -limit, limit).astype(held_as)


def gaussian_with(key, extent, width, most, shards, heavy, kind=jnp.bfloat16):
    values = width * jax.random.normal(key, extent, jnp.float32)
    if shards:
        values = values * block_scale(key, extent, shards, -0.22, 0.18)
    return jnp.clip(with_spikes(values, jax.random.fold_in(key, 3), *heavy), -most, most).astype(kind)


def setup_inputs(seed: int = 0) -> dict:
    splits = jax.random.split(jax.random.key(seed), 10)
    merged_grad = noise(splits[0], (TOKENS, OUTW), 1.0, 6.0, ((0, 32),))
    merged_owner_keys = jax.random.split(jax.random.fold_in(splits[1], 1), TOKENS // G_DEV)
    merged_owner_turns = jax.random.permutation(jax.random.fold_in(splits[1], 3), TOKENS // G_DEV)
    merged_owner = jax.vmap(lambda own, number: routed_block(jax.random.fold_in(splits[1], 2), own, number, G_DEV, N_CTX, 1, CAP, 2))(merged_owner_keys, merged_owner_turns).reshape((TOKENS, 1))
    merger_pre = gaussian_with(splits[2], (ALLSLOTS, HID), 1.0, 6.0, ((0, 32),), (0, 1, 32, 2.75))
    fc2_weight = noise(splits[3], (HID, OUTW), HID ** -0.5, 0.125, ((0, 8),))
    query = draw_query(jax.random.fold_in(splits[9], 71), 0)
    key_states = draw_key_states(jax.random.fold_in(splits[9], 71), 0)
    value_states = noise(splits[6], (PATCHES, D), 1.0, 6.0, ((0, 32),))
    out_grad = noise(splits[7], (PATCHES, D), 1.0, 6.0, ((0, 32),))
    position = draw_position(jax.random.fold_in(splits[9], 71), 0)
    return {"merged_grad": merged_grad, "merged_owner": merged_owner, "merger_pre": merger_pre, "fc2_weight": fc2_weight, "query": query, "key_states": key_states, "value_states": value_states, "out_grad": out_grad, "position": position}


def rope_angles(position, head_size):
    quarter = head_size // 4
    freq = 1.0 / (10000.0 ** (jnp.arange(quarter, dtype=jnp.float32) * (4.0 / head_size)))
    rows = position[0].astype(jnp.float32)[:, None] * freq[None, :]
    cols = position[1].astype(jnp.float32)[:, None] * freq[None, :]
    return jnp.concatenate([rows, cols], axis=1)


def rotate(values, angles, sign):
    half = values.shape[-1] // 2
    cosine = jnp.cos(angles)[:, None, :]
    sine = sign * jnp.sin(angles)[:, None, :]
    first = values[..., :half]
    second = values[..., half:]
    return jnp.concatenate([first * cosine - second * sine, second * cosine + first * sine], axis=-1)


def attention_block(query, key_states, value_states, out_grad, position):
    count = query.shape[0]
    windows = count // WIN
    angles = rope_angles(position, HEAD)
    shaped = (count, HEADS, HEAD)
    grouped = (windows, WIN, HEADS, HEAD)
    q_rot = rotate(query.astype(jnp.float32).reshape(shaped), angles, 1.0).astype(jnp.bfloat16)
    k_rot = rotate(key_states.astype(jnp.float32).reshape(shaped), angles, 1.0).astype(jnp.bfloat16)
    q_full = lax.optimization_barrier(q_rot).reshape(grouped).astype(jnp.float32)
    k_full = lax.optimization_barrier(k_rot).reshape(grouped).astype(jnp.float32)
    v_full = value_states.reshape(grouped).astype(jnp.float32)
    g_full = out_grad.reshape(grouped).astype(jnp.float32)
    factor = HEAD ** -0.5
    scores = jnp.einsum("wqhd,wkhd->whqk", q_full, k_full) * factor
    probs = jax.nn.softmax(scores, axis=-1)
    probs_b = lax.optimization_barrier(probs.astype(jnp.bfloat16)).astype(jnp.float32)
    output = jnp.einsum("whqk,wkhd->wqhd", probs_b, v_full)
    value_grad = jnp.einsum("whqk,wqhd->wkhd", probs_b, g_full).astype(jnp.bfloat16)
    prob_grad = jnp.einsum("wqhd,wkhd->whqk", g_full, v_full)
    delta = jnp.transpose(jnp.sum(g_full * output, axis=-1), (0, 2, 1))[..., None]
    score_grad = (probs * (prob_grad - delta)).astype(jnp.bfloat16)
    score_full = lax.optimization_barrier(score_grad).astype(jnp.float32)
    q_grad = jnp.einsum("whqk,wkhd->wqhd", score_full, k_full) * factor
    k_grad = jnp.einsum("whqk,wqhd->wkhd", score_full, q_full) * factor
    query_grad = rotate(q_grad.reshape(shaped), angles, -1.0).astype(jnp.bfloat16).reshape(count, D)
    key_grad = rotate(k_grad.reshape(shaped), angles, -1.0).astype(jnp.bfloat16).reshape(count, D)
    return query_grad, key_grad, value_grad.reshape(count, D)


def reference(merged_grad, merged_owner, merger_pre, fc2_weight, query, key_states, value_states, out_grad, position):
    group_rows = N_CTX * G_DEV
    owner = merged_owner[:, 0].reshape(N_DP, group_rows)
    owners = jnp.arange(N_CTX, dtype=jnp.int32)
    onehot = (owner[:, :, None] == owners[None, None, :]).astype(jnp.int32)
    running = jnp.cumsum(onehot, axis=1, dtype=jnp.int32)
    slot = jnp.sum(running * onehot, axis=2, dtype=jnp.int32) - 1
    group = jnp.arange(N_DP, dtype=jnp.int32)[:, None]
    target = ((group * N_CTX + owner) * SLOTS + slot).reshape(-1).astype(jnp.int32)
    slotted = jnp.zeros((N_DP * N_CTX * SLOTS, OUTW), jnp.bfloat16).at[target].set(merged_grad)

    def merger_group(carry, items):
        slotted_part, pre_part = items
        pre = pre_part.astype(jnp.float32)
        cdf = 0.5 * (1.0 + lax.erf(pre * (0.5 ** 0.5)))
        act = (pre * cdf).astype(jnp.bfloat16)
        slope = cdf + pre * jnp.exp(-0.5 * pre * pre) * ((2.0 * math.pi) ** -0.5)
        linear = jnp.dot(slotted_part, fc2_weight.T, preferred_element_type=jnp.float32)
        hidden = (linear * slope).astype(jnp.bfloat16)
        carry = carry + jnp.dot(act.T, slotted_part, preferred_element_type=jnp.float32)
        return carry, hidden

    weight_sum, hidden = lax.scan(
        merger_group,
        jnp.zeros((HID, OUTW), jnp.float32),
        (slotted.reshape(N_DP * N_CTX, SLOTS, OUTW), merger_pre.reshape(N_DP * N_CTX, SLOTS, HID)),
    )
    hidden_grad = hidden.reshape(N_DP * N_CTX * SLOTS, HID)
    weight_grad = weight_sum * (TOKENS ** -0.5)

    blocks = PATCHES // PATCH_DEV
    stacked = (
        query.reshape(blocks, PATCH_DEV, D),
        key_states.reshape(blocks, PATCH_DEV, D),
        value_states.reshape(blocks, PATCH_DEV, D),
        out_grad.reshape(blocks, PATCH_DEV, D),
        jnp.transpose(position.reshape(2, blocks, PATCH_DEV), (1, 0, 2)),
    )

    def one_block(items):
        return attention_block(items[0], items[1], items[2], items[3], items[4])

    query_grad, key_grad, value_grad = lax.map(one_block, stacked)
    return (
        hidden_grad,
        weight_grad,
        query_grad.reshape(PATCHES, D),
        key_grad.reshape(PATCHES, D),
        value_grad.reshape(PATCHES, D),
    )
```

```python
import functools
import math

import jax
import jax.numpy as jnp
from jax import lax
from jax.experimental import pallas as pl
from jax.experimental.pallas import tpu as pltpu
from jax.sharding import PartitionSpec as P

HEAD = 80
WIN = 64
LANES = 128
SIDES = 2
F32 = jnp.float32
BF16 = jnp.bfloat16
MESH = pl.DeviceIdType.MESH
NT = (((1,), (1,)), ((), ()))
TN = (((0,), (0,)), ((), ()))
NN = (((1,), (0,)), ((), ()))


def dot(a, b, dims=NN):
    return lax.dot_general(a, b, dims, preferred_element_type=F32)


def spread(table, width):
    shape = (LANES, width)
    lane = lax.broadcasted_iota(jnp.int32, shape, 1) % HEAD
    pick = (lane == lax.broadcasted_iota(jnp.int32, shape, 0)).astype(F32).astype(BF16)
    high = table.astype(BF16)
    rest = table - high.astype(F32)
    mid = rest.astype(BF16)
    low = (rest - mid.astype(F32)).astype(BF16)
    return dot(high, pick) + dot(mid, pick) + dot(low, pick)


def rope_tables(pos_ref, freq_ref, c_ref, s_ref):
    count = pos_ref.shape[1]
    half, quarter = HEAD // 2, HEAD // 4
    unit = lax.broadcasted_iota(jnp.int32, (LANES, count), 0)
    rows = pos_ref[0:1, :].astype(F32)
    cols = pos_ref[1:2, :].astype(F32)
    freq = jnp.transpose(jnp.broadcast_to(freq_ref[...], (count, LANES)))
    angles = jnp.where(unit % half < quarter, rows, cols) * freq
    c_ref[...] = jnp.transpose(jnp.cos(angles))
    s_ref[...] = jnp.transpose(jnp.where(unit < half, -1.0, 1.0) * jnp.sin(angles))


def attention_part(at, over, refs, c_ref, s_ref, outs):
    q_ref, k_ref, v_ref, g_ref = refs
    dq_ref, dk_ref, dv_ref = outs
    width = over.size
    heads = width // HEAD
    half = HEAD // 2
    cosine = spread(c_ref[at, :], width)
    sine = spread(s_ref[at, :], width)
    lane = lax.broadcasted_iota(jnp.int32, (WIN, width), 1)
    first = lane % HEAD < half

    def swap(x):
        return jnp.where(first, pltpu.roll(x, width - half, 1), pltpu.roll(x, half, 1))

    def rotated(x):
        return (x * cosine + swap(x) * sine).astype(BF16)

    def unrotated(x):
        return (x * cosine - swap(x) * sine).astype(BF16)

    q = rotated(q_ref[at, over].astype(F32))
    k = rotated(k_ref[at, over].astype(F32))
    v = v_ref[at, over]
    g = g_ref[at, over]
    factor = HEAD ** (-0.5)
    dq, dk, dv = {}, {}, {}

    def add(into, tile, value):
        for i in range(value.shape[1] // LANES):
            part = value[:, i * LANES : (i + 1) * LANES]
            into[tile + i] = into[tile + i] + part if tile + i in into else part

    for head in range(heads):
        tile = head * HEAD // LANES
        end = -(-(head + 1) * HEAD // LANES)
        lo, hi = tile * LANES, end * LANES
        here = lax.broadcasted_iota(jnp.int32, (1, hi - lo), 1) + lo
        mask = ((here >= head * HEAD) & (here < (head + 1) * HEAD)).astype(F32).astype(BF16)
        qm = q[:, lo:hi] * mask
        km = k[:, lo:hi] * mask
        gm = g[:, lo:hi] * mask
        scores = dot(qm, k[:, lo:hi], NT) * factor
        weight = jnp.exp(scores - jnp.max(scores, axis=1, keepdims=True))
        probs = weight * (1.0 / jnp.sum(weight, axis=1, keepdims=True))
        probs_b = probs.astype(BF16)
        prob_grad = dot(gm, v[:, lo:hi], NT)
        delta = jnp.sum(probs_b.astype(F32) * prob_grad, axis=1, keepdims=True)
        score_grad = (probs * (prob_grad - delta)).astype(BF16)
        add(dv, tile, dot(probs_b, gm, TN))
        add(dq, tile, dot(score_grad, km, NN))
        add(dk, tile, dot(score_grad, qm, TN))

    def joined(parts):
        return jnp.concatenate([parts[i] for i in range(width // LANES)], axis=1)

    dq_ref[at, over] = unrotated(joined(dq) * factor)
    dk_ref[at, over] = unrotated(joined(dk) * factor)
    dv_ref[at, over] = joined(dv).astype(BF16)


def fused_kernel(
    n,
    replicas,
    m_hbm,
    o_ref,
    p_hbm,
    w_hbm,
    q_hbm,
    k_hbm,
    v_hbm,
    g_hbm,
    pos_ref,
    freq_ref,
    h_hbm,
    wg_hbm,
    dq_hbm,
    dk_hbm,
    dv_hbm,
    mall,
    owners,
    pre,
    slope,
    pre_send,
    pre_got,
    fall,
    w_ref,
    code,
    slotted,
    hid,
    hid_out,
    hid_got,
    h_ref,
    full,
    part,
    core_got,
    x_got,
    wg_ref,
    q_ref,
    k_ref,
    v_ref,
    g_ref,
    dq_ref,
    dk_ref,
    dv_ref,
    c_ref,
    s_ref,
    m_recv,
    up_sem,
    down_sem,
    side_sem,
    o_send,
    o_recv,
    p_send,
    p_recv,
    f_recv,
    mirror_sem,
    fup_sem,
    fdown_sem,
    fside_sem,
    fx_sem,
    fcore_sem,
    h_send,
    h_recv,
    c_send,
    c_recv,
    x_send,
    x_recv,
    local_sem,
    out_sem,
):
    line = n // SIDES
    near = n // 2
    near_line = line // 2
    rows_here, width = m_hbm.shape
    slots, units = pre.shape
    mine = units // n
    parts = w_hbm.shape[0]
    shared = parts > 1
    block = SIDES * rows_here
    patches, features = q_ref.shape
    chips = replicas // 2
    me = lax.axis_index("ctx")
    rep = lax.axis_index("dp")
    a, b = me // SIDES, me % SIDES
    side, row = a // near_line, a % near_line
    here = me % near
    mirror = (me + near) % n
    partner = rep // 2 * 2 + 1 - rep % 2
    core = rep % 2
    q_own = rep if shared else 0
    q_far = (rep + 2) % replicas if shared else 0

    barrier = pltpu.get_barrier_semaphore()
    for r in range(1, n):
        pl.semaphore_signal(barrier, inc=1, device_id={"dp": rep, "ctx": (me + r) % n}, device_id_type=MESH)
    pl.semaphore_signal(barrier, inc=1, device_id={"dp": partner, "ctx": me}, device_id_type=MESH)
    for r in range(1, chips):
        pl.semaphore_signal(
            barrier, inc=1, device_id={"dp": (rep + 2 * r) % replicas, "ctx": me}, device_id_type=MESH
        )
    locals_ = [
        pltpu.make_async_copy(p_hbm, pre, local_sem.at[0]),
        pltpu.make_async_copy(q_hbm, q_ref, local_sem.at[1]),
        pltpu.make_async_copy(k_hbm, k_ref, local_sem.at[2]),
        pltpu.make_async_copy(v_hbm, v_ref, local_sem.at[3]),
        pltpu.make_async_copy(g_hbm, g_ref, local_sem.at[4]),
        pltpu.make_async_copy(m_hbm, mall.at[me], local_sem.at[5]),
        pltpu.make_async_copy(w_hbm, w_ref, local_sem.at[6]),
        pltpu.make_async_copy(o_ref, owners.at[me], local_sem.at[7]),
    ]
    for copy in locals_:
        copy.start()
    pl.semaphore_wait(barrier, n - 1 + chips)

    def send(src, dst, send_sem, recv_sem, ctx=None, dp=None):
        where = {"dp": rep if dp is None else dp, "ctx": me if ctx is None else ctx}
        return pltpu.make_async_remote_copy(
            src_ref=src,
            dst_ref=dst,
            send_sem=send_sem,
            recv_sem=recv_sem,
            device_id=where,
            device_id_type=MESH,
        )

    def owner_copy(r):
        return send(o_ref, owners.at[me], o_send.at[r - 1], o_recv.at[r - 1], ctx=(me + r) % n)

    def unit_rows(peer):
        return pre_send.at[pl.ds(pl.multiple_of(peer * mine, 16), mine), :]

    def pre_copy(r):
        peer = (me + r) % n
        return send(unit_rows(peer), pre_got.at[me], p_send.at[r - 1], p_recv.at[r - 1], ctx=peer)

    def hidden_copy(r):
        to = (here + r) % near
        return send(
            hid_out.at[to], hid_got.at[here], h_send.at[r - 1], h_recv.at[r - 1], ctx=side * near + to
        )

    def up_copy(t, ref):
        at = (a - t) * SIDES + b
        return send(ref, mall.at[at], up_sem.at[t], m_recv.at[at], ctx=me + SIDES)

    def down_copy(t, ref):
        at = (a + t) * SIDES + b
        return send(ref, mall.at[at], down_sem.at[t], m_recv.at[at], ctx=me - SIDES)

    def side_copy(at, ref):
        src = at * SIDES + b
        return send(ref, mall.at[src], side_sem.at[at], m_recv.at[src], ctx=a * SIDES + 1 - b)

    def m_arrived(src):
        send(mall.at[src], mall.at[src], up_sem.at[0], m_recv.at[src], ctx=a * SIDES + 1 - b).wait_recv()

    def mirror_copy():
        return send(
            w_hbm.at[q_own], fall.at[here, q_own], mirror_sem.at[0], f_recv.at[here, q_own], ctx=mirror
        )

    def fup_copy(t):
        at = (row - t) * SIDES + b
        ref = fall.at[at, q_own]
        return send(ref, ref, fup_sem.at[t], f_recv.at[at, q_own], ctx=me + SIDES)

    def fdown_copy(t):
        at = (row + t) * SIDES + b
        ref = fall.at[at, q_own]
        return send(ref, ref, fdown_sem.at[t], f_recv.at[at, q_own], ctx=me - SIDES)

    def fside_copy(at):
        src = at * SIDES + b
        ref = fall.at[src, q_own]
        return send(ref, ref, fside_sem.at[at], f_recv.at[src, q_own], ctx=a * SIDES + 1 - b)

    def fx_copy(src):
        ref = fall.at[src, q_own]
        return send(ref, ref, fx_sem.at[src], f_recv.at[src, q_own], dp=q_far)

    def fcore_copy(src, which):
        at = (q_own, q_far)[which]
        ref = fall.at[src, at]
        return send(ref, ref, fcore_sem.at[src, which], f_recv.at[src, at], dp=partner)

    def f_arrived(src, at):
        ref = fall.at[src, at]
        send(ref, ref, fup_sem.at[0], f_recv.at[src, at], ctx=a * SIDES + 1 - b).wait_recv()

    def core_copy(x):
        return send(
            part.at[2 * x + 1 - core], core_got.at[x], c_send.at[x], c_recv.at[x], dp=partner
        )

    def x_copy(r):
        peer = (rep + 2 * r) % replicas
        return send(part.at[peer], x_got.at[r - 1], x_send.at[r - 1], x_recv.at[r - 1], dp=peer)

    def when(condition, body):
        pl.when(condition)(body)

    for r in range(1, n):
        owner_copy(r).start()
    when(a + 1 < line, lambda: up_copy(0, m_hbm).start())
    when(a > 0, lambda: down_copy(0, m_hbm).start())
    side_copy(a, m_hbm).start()
    mirror_copy().start()

    locals_[0].wait()

    def turn(j, carry):
        over = pl.ds(pl.multiple_of(j * LANES, LANES), LANES)
        pre_send[over, :] = jnp.transpose(pre[:, over].astype(F32)).astype(BF16)
        return carry

    lax.fori_loop(0, units // LANES, turn, 0)
    own_pre = pltpu.make_async_copy(unit_rows(me), pre_got.at[me], local_sem.at[8])
    own_pre.start()
    rope_tables(pos_ref, freq_ref, c_ref, s_ref)
    full[...] = jnp.zeros_like(full)
    slotted[...] = jnp.zeros_like(slotted)
    for copy in locals_[1:5]:
        copy.wait()

    def both(t, at, count, body):
        if t == 0:
            body(at, None)
        else:
            when(at - t >= 0, lambda: body(at - t, True))
            when(at + t < count, lambda: body(at + t, False))

    def send_pre():
        for r in range(1, n):
            pre_copy(r).start()

    def token_event(t):
        def body(at, below):
            src = at * SIDES + b
            ref = mall.at[src]
            m_arrived(src)
            if below:
                when(a + 1 < line, lambda: up_copy(t, ref).start())
            else:
                when(a > 0, lambda: down_copy(t, ref).start())
            side_copy(at, ref).start()

        both(t, a, line, body)

    def across(src):
        if shared:
            fx_copy(src).start()
            fcore_copy(src, 0).start()

    def weight_event(t):
        def body(at, below):
            src = at * SIDES + b
            f_arrived(src, q_own)
            if below is not False:
                when(row + 1 < near_line, lambda: fup_copy(t).start())
            if below is not True:
                when(row > 0, lambda: fdown_copy(t).start())
            fside_copy(at).start()
            across(src)

        both(t, row, near_line, body)

    def weight_side_event(t):
        def body(at, below):
            src = at * SIDES + 1 - b
            f_arrived(src, q_own)
            across(src)

        both(t, row, near_line, body)

    def weight_far_event(t, other):
        def body(at, below):
            src = at * SIDES + (1 - b if other else b)
            if shared:
                f_arrived(src, q_far)
                fcore_copy(src, 1).start()

        both(t, row, near_line, body)

    def event(kind, *given):
        return functools.partial(kind, *given)

    order = [(1, event(token_event, 1))]
    if line > 2:
        order += [(3, event(token_event, 2))]
    order += [(3, send_pre)]
    for t in range(near_line):
        order += [(4 + 2 * t, event(weight_event, t)), (4 + 2 * t, event(weight_side_event, t))]
    for t in range(3, line):
        order += [(8, event(token_event, t))]
    for t in range(near_line):
        order += [(6 + 2 * t, event(weight_far_event, t, False)), (6 + 2 * t, event(weight_far_event, t, True))]

    halves = 2
    span = features // halves
    steps = patches // WIN * halves

    def attend(i, carry):
        at = pl.ds(pl.multiple_of(i // halves * WIN, WIN), WIN)
        over = pl.ds(pl.multiple_of(i % halves * span, LANES), span)
        attention_part(
            at, over, (q_ref, k_ref, v_ref, g_ref), c_ref, s_ref, (dq_ref, dk_ref, dv_ref)
        )
        for step in range(steps):
            todo = [run for index, run in order if index == step]
            if todo:
                when(i == step, lambda todo=todo: [run() for run in todo] and None)
        return carry

    lax.fori_loop(0, steps, attend, 0)
    outs = [
        pltpu.make_async_copy(dq_ref, dq_hbm, out_sem.at[0]),
        pltpu.make_async_copy(dk_ref, dk_hbm, out_sem.at[1]),
        pltpu.make_async_copy(dv_ref, dv_hbm, out_sem.at[2]),
    ]
    for copy in outs:
        copy.start()

    far = (1 - side) * (units // 2)

    def incline(j, carry):
        x = pre[:, pl.ds(pl.multiple_of(far + j * LANES, LANES), LANES)].astype(F32)
        cdf = 0.5 * (1.0 + lax.erf(x * 0.5**0.5))
        slope[:, pl.ds(pl.multiple_of(j * LANES, LANES), LANES)] = cdf + x * jnp.exp(-0.5 * x * x) * (
            2.0 * math.pi
        ) ** (-0.5)
        return carry

    lax.fori_loop(0, units // 2 // LANES, incline, 0)

    for copy in locals_[5:]:
        copy.wait()
    for r in range(1, n):
        owner_copy(r).wait()
    padded = -(-n // 16) * 16
    earlier = lax.broadcasted_iota(jnp.int32, (rows_here, rows_here), 0) < lax.broadcasted_iota(
        jnp.int32, (rows_here, rows_here), 1
    )
    earlier = earlier.astype(F32).astype(BF16)
    names = lax.broadcasted_iota(jnp.int32, (padded, rows_here), 0)
    base = jnp.zeros((padded, 1), F32)
    for s in range(n):
        onehot = (names == owners[s]).astype(F32)
        count = dot(onehot.astype(BF16), earlier) + base
        position = jnp.sum(onehot * (count + names.astype(F32) * float(slots)), axis=0, keepdims=True)
        base = base + jnp.sum(onehot, axis=1, keepdims=True)
        lo = s % SIDES * rows_here
        code[s // SIDES, :, lo : lo + rows_here] = jnp.broadcast_to(position, (8, rows_here))
    standing = lax.broadcasted_iota(jnp.int32, (slots, block), 0).astype(F32)

    def landing(o, t):
        first = (o * slots).astype(F32)
        return (standing == code[t, 0:1, :] - first).astype(F32).astype(BF16)

    for index, run in sorted((pair for pair in order if pair[0] >= steps), key=lambda pair: pair[0]):
        run()
    for r in range(1, n):
        pre_copy(r).wait()
    own_pre.wait()

    def tokens(d, carry):
        low = jnp.where(d <= a, a - d, d)
        flip = line - 1 - a
        high = line - 1 - jnp.where(d <= flip, flip - d, d)
        t = jnp.where(side == 0, low, high)
        m_arrived(t * SIDES + 1 - b)

        def gather(o, total):
            return total + dot(pre_got[o], landing(o, t))

        x = lax.fori_loop(0, n, gather, jnp.zeros((mine, block), F32))
        cdf = 0.5 * (1.0 + lax.erf(x * 0.5**0.5))
        incline = cdf + x * jnp.exp(-0.5 * x * x) * (2.0 * math.pi) ** (-0.5)
        rows = jnp.concatenate([mall[t * SIDES + i] for i in range(SIDES)], axis=0)
        hid[t] = (dot(w_ref[...].reshape(mine, width), rows, NT) * incline).astype(BF16)
        full[...] += dot((x * cdf).astype(BF16), rows)
        slotted[...] += dot(landing(me, t), rows).astype(BF16)
        return carry

    lax.fori_loop(0, line, tokens, 0)

    piece = width // replicas
    for d in range(replicas):
        lo = d * piece // LANES * LANES
        hi = -(-(d + 1) * piece // LANES) * LANES
        shift = d * piece - lo
        value = full[:, lo:hi]
        if shift:
            value = pltpu.roll(value, hi - lo - shift, 1)
        part[d] = value[:, :piece]
    for x in range(chips):
        core_copy(x).start()

    def outgoing(i, carry):
        def gather(t, total):
            return total + dot(hid[t], landing(side * near + i, t), NT)

        hid_out[i] = lax.fori_loop(0, line, gather, jnp.zeros((mine, slots), F32)).astype(BF16)
        return carry

    lax.fori_loop(0, near, outgoing, 0)
    for r in range(1, near):
        hidden_copy(r).start()
    own_hidden = pltpu.make_async_copy(hid_out.at[here], hid_got.at[here], local_sem.at[9])
    own_hidden.start()

    for x in range(chips):
        core_copy(x).wait()
    for x in range(chips):
        part[2 * x + core] = part[2 * x + core] + core_got[x]
    for r in range(1, chips):
        x_copy(r).start()

    groups = next(g for g in range(near_line, 0, -1) if near_line % g == 0 and units // 2 // g % LANES == 0)
    run, each = near // groups, units // 2 // groups

    def h_copy(g, start):
        over = pl.ds(pl.multiple_of(start + g * each, LANES), each)
        return pltpu.make_async_copy(h_ref.at[:, over], h_hbm.at[:, over], out_sem.at[3])

    def linear(g, carry):
        if shared:

            def await_rest(i, carry):
                for other in (partner, (partner + 2) % replicas):
                    f_arrived(g * run + i, other)
                return carry

            lax.fori_loop(0, run, await_rest, 0)
        weight = fall[pl.ds(g * run, run)].reshape(each, width)
        over = pl.ds(pl.multiple_of(g * each, LANES), each)
        to = pl.ds(pl.multiple_of(far + g * each, LANES), each)
        h_ref[:, to] = (dot(slotted[...], weight, NT) * slope[:, over]).astype(BF16)
        return carry

    lax.fori_loop(0, groups, linear, 0)

    own_hidden.wait()
    for r in range(1, near):
        hidden_copy(r).wait()
    spot = lax.broadcasted_iota(jnp.int32, (slots, slots), 0) == lax.broadcasted_iota(
        jnp.int32, (slots, slots), 1
    )
    spot = spot.astype(F32).astype(BF16)

    def settle(g, carry):
        rows = hid_got[pl.ds(g * run, run)].reshape(each, slots)
        to = pl.ds(pl.multiple_of(side * (units // 2) + g * each, LANES), each)
        h_ref[:, to] = dot(spot, rows, NT).astype(BF16)
        return carry

    lax.fori_loop(0, groups, settle, 0)
    outs.append(pltpu.make_async_copy(h_ref, h_hbm, out_sem.at[3]))
    outs[-1].start()

    total = part[rep]
    for r in range(1, chips):
        x_copy(r).wait()
        total = total + x_got[r - 1]
    wg_ref[...] = total * (rows_here * n * replicas) ** (-0.5)
    outs.append(pltpu.make_async_copy(wg_ref, wg_hbm, out_sem.at[4]))
    outs[-1].start()

    def sent(t, carry):
        @pl.when((a - t >= 0) & (a + 1 < line))
        def _():
            up_copy(t, mall.at[me]).wait_send()

        @pl.when((a + t < line) & (a > 0))
        def _():
            down_copy(t, mall.at[me]).wait_send()

        side_copy(t, mall.at[me]).wait_send()
        return carry

    lax.fori_loop(0, line, sent, 0)
    mirror_copy().wait_send()

    def weight_sent(t, carry):
        @pl.when((row - t >= 0) & (row + 1 < near_line))
        def _():
            fup_copy(t).wait_send()

        @pl.when((row + t < near_line) & (row > 0))
        def _():
            fdown_copy(t).wait_send()

        fside_copy(t).wait_send()
        return carry

    lax.fori_loop(0, near_line, weight_sent, 0)
    if shared:

        def passed(src, carry):
            fx_copy(src).wait_send()
            fcore_copy(src, 0).wait_send()
            fcore_copy(src, 1).wait_send()
            return carry

        lax.fori_loop(0, near, passed, 0)
    for copy in outs:
        copy.wait()


def finish_kernel(*refs):
    ins, outs, held = refs[:5], refs[5:10], refs[10:15]
    in_sem, out_sem = refs[15:]
    first = [pltpu.make_async_copy(ins[i], held[i], in_sem.at[i]) for i in range(5)]
    second = [pltpu.make_async_copy(held[i], outs[i], out_sem.at[i]) for i in range(5)]
    for copy in first:
        copy.start()
    for i in range(5):
        first[i].wait()
        second[i].start()
    for copy in second:
        copy.wait()


def fused(merged_grad, merged_owner, merger_pre, fc2_weight, query, key_states, value_states, out_grad, position):
    rows_here, width = merged_grad.shape
    n, replicas = lax.axis_size("ctx"), lax.axis_size("dp")
    slots, units = merger_pre.shape
    mine = units // n
    line = n // SIDES
    near = n // 2
    near_line = line // 2
    block = SIDES * rows_here
    piece = width // replicas
    chips = replicas // 2
    parts = replicas if chips == 2 and mine % (16 * replicas) == 0 else 1
    quarter = HEAD // 4
    freq = 1.0 / 10000.0 ** (jnp.arange(quarter, dtype=F32) * (4.0 / HEAD))
    freq = jnp.concatenate([freq] * 4 + [jnp.zeros((LANES - HEAD,), F32)]).reshape(1, LANES)
    vmem = pl.BlockSpec(memory_space=pltpu.VMEM)
    hbm = pl.BlockSpec(memory_space=pl.ANY)
    dma = pltpu.SemaphoreType.DMA
    like = jax.ShapeDtypeStruct(query.shape, BF16)
    shapes = [
        jax.ShapeDtypeStruct((slots, units), BF16),
        jax.ShapeDtypeStruct((mine, piece), F32),
        like,
        like,
        like,
    ]
    results = pl.pallas_call(
        functools.partial(fused_kernel, n, replicas),
        in_specs=[hbm, vmem] + [hbm] * 6 + [vmem] * 2,
        out_specs=[hbm] * 5,
        out_shape=shapes,
        scratch_shapes=[
            pltpu.VMEM((n, rows_here, width), BF16),
            pltpu.VMEM((n, 1, rows_here), jnp.int32),
            pltpu.VMEM((slots, units), BF16),
            pltpu.VMEM((slots, units // 2), F32),
            pltpu.VMEM((units, slots), BF16),
            pltpu.VMEM((n, mine, slots), BF16),
            pltpu.VMEM((near, parts, mine // parts, width), BF16),
            pltpu.VMEM((parts, mine // parts, width), BF16),
            pltpu.VMEM((line, 8, block), F32),
            pltpu.VMEM((slots, width), BF16),
            pltpu.VMEM((line, mine, block), BF16),
            pltpu.VMEM((near, mine, slots), BF16),
            pltpu.VMEM((near, mine, slots), BF16),
            pltpu.VMEM((slots, units), BF16),
            pltpu.VMEM((mine, width), F32),
            pltpu.VMEM((replicas, mine, piece), F32),
            pltpu.VMEM((chips, mine, piece), F32),
            pltpu.VMEM((max(chips - 1, 1), mine, piece), F32),
            pltpu.VMEM((mine, piece), F32),
        ]
        + [pltpu.VMEM(query.shape, BF16)] * 7
        + [
            pltpu.VMEM((query.shape[0], LANES), F32),
            pltpu.VMEM((query.shape[0], LANES), F32),
            dma((n,)),
            dma((line,)),
            dma((line,)),
            dma((line,)),
            dma((n - 1,)),
            dma((n - 1,)),
            dma((n - 1,)),
            dma((n - 1,)),
            dma((near, parts)),
            dma((1,)),
            dma((near_line,)),
            dma((near_line,)),
            dma((near_line,)),
            dma((near,)),
            dma((near, 2)),
            dma((near - 1,)),
            dma((near - 1,)),
            dma((chips,)),
            dma((chips,)),
            dma((max(chips - 1, 1),)),
            dma((max(chips - 1, 1),)),
            dma((10,)),
            dma((5,)),
        ],
        compiler_params=pltpu.CompilerParams(
            collective_id=0, has_side_effects=True, vmem_limit_bytes=60 * 2**20
        ),
        name="fused",
    )(
        merged_grad,
        merged_owner.reshape(1, rows_here),
        merger_pre,
        fc2_weight.reshape(parts, mine // parts, width),
        query,
        key_states,
        value_states,
        out_grad,
        position,
        freq,
    )
    return tuple(
        pl.pallas_call(
            finish_kernel,
            in_specs=[hbm] * 5,
            out_specs=[hbm] * 5,
            out_shape=shapes,
            scratch_shapes=[pltpu.VMEM(shape.shape, shape.dtype) for shape in shapes] + [dma((5,)), dma((5,))],
            name="finish",
        )(*results)
    )


def solution(mesh):
    every = P(("dp", "ctx"), None)
    return jax.shard_map(
        fused,
        mesh=mesh,
        in_specs=(every, every, every, P("ctx", None)) + (every,) * 4 + (P(None, ("dp", "ctx")),),
        out_specs=(every, P("ctx", "dp")) + (every,) * 3,
        check_vma=False,
    )
```

```python
import functools
import math

import jax
import jax.numpy as jnp
from jax import lax
from jax.experimental import pallas as pl
from jax.experimental.pallas import tpu as pltpu
from jax.sharding import PartitionSpec as P

HEAD = 80
WIN = 64
LANES = 128
SIDES = 2
F32 = jnp.float32
BF16 = jnp.bfloat16
MESH = pl.DeviceIdType.MESH
NT = (((1,), (1,)), ((), ()))
TN = (((0,), (0,)), ((), ()))
NN = (((1,), (0,)), ((), ()))


def dot(a, b, dims=NN):
    return lax.dot_general(a, b, dims, preferred_element_type=F32)


def spread(table, width):
    shape = (LANES, width)
    lane = lax.broadcasted_iota(jnp.int32, shape, 1) % HEAD
    pick = (lane == lax.broadcasted_iota(jnp.int32, shape, 0)).astype(F32).astype(BF16)
    high = table.astype(BF16)
    rest = table - high.astype(F32)
    mid = rest.astype(BF16)
    low = (rest - mid.astype(F32)).astype(BF16)
    return dot(high, pick) + dot(mid, pick) + dot(low, pick)


def rope_tables(pos_ref, freq_ref, c_ref, s_ref):
    count = pos_ref.shape[1]
    half, quarter = HEAD // 2, HEAD // 4
    unit = lax.broadcasted_iota(jnp.int32, (LANES, count), 0)
    rows = pos_ref[0:1, :].astype(F32)
    cols = pos_ref[1:2, :].astype(F32)
    freq = jnp.transpose(jnp.broadcast_to(freq_ref[...], (count, LANES)))
    angles = jnp.where(unit % half < quarter, rows, cols) * freq
    c_ref[...] = jnp.transpose(jnp.cos(angles))
    s_ref[...] = jnp.transpose(jnp.where(unit < half, -1.0, 1.0) * jnp.sin(angles))


def attention_part(at, over, refs, c_ref, s_ref, outs):
    q_ref, k_ref, v_ref, g_ref = refs
    dq_ref, dk_ref, dv_ref = outs
    width = over.size
    heads = width // HEAD
    half = HEAD // 2
    cosine = spread(c_ref[at, :], width)
    sine = spread(s_ref[at, :], width)
    lane = lax.broadcasted_iota(jnp.int32, (WIN, width), 1)
    first = lane % HEAD < half

    def swap(x):
        return jnp.where(first, pltpu.roll(x, width - half, 1), pltpu.roll(x, half, 1))

    def rotated(x):
        return (x * cosine + swap(x) * sine).astype(BF16)

    def unrotated(x):
        return (x * cosine - swap(x) * sine).astype(BF16)

    q = rotated(q_ref[at, over].astype(F32))
    k = rotated(k_ref[at, over].astype(F32))
    v = v_ref[at, over]
    g = g_ref[at, over]
    factor = HEAD ** (-0.5)
    dq, dk, dv = {}, {}, {}

    def add(into, tile, value):
        for i in range(value.shape[1] // LANES):
            part = value[:, i * LANES : (i + 1) * LANES]
            into[tile + i] = into[tile + i] + part if tile + i in into else part

    for head in range(heads):
        tile = head * HEAD // LANES
        end = -(-(head + 1) * HEAD // LANES)
        lo, hi = tile * LANES, end * LANES
        here = lax.broadcasted_iota(jnp.int32, (1, hi - lo), 1) + lo
        mask = ((here >= head * HEAD) & (here < (head + 1) * HEAD)).astype(F32).astype(BF16)
        qm = q[:, lo:hi] * mask
        km = k[:, lo:hi] * mask
        gm = g[:, lo:hi] * mask
        scores = dot(qm, k[:, lo:hi], NT) * factor
        weight = jnp.exp(scores - jnp.max(scores, axis=1, keepdims=True))
        probs = weight * (1.0 / jnp.sum(weight, axis=1, keepdims=True))
        probs_b = probs.astype(BF16)
        prob_grad = dot(gm, v[:, lo:hi], NT)
        delta = jnp.sum(probs_b.astype(F32) * prob_grad, axis=1, keepdims=True)
        score_grad = (probs * (prob_grad - delta)).astype(BF16)
        add(dv, tile, dot(probs_b, gm, TN))
        add(dq, tile, dot(score_grad, km, NN))
        add(dk, tile, dot(score_grad, qm, TN))

    def joined(parts):
        return jnp.concatenate([parts[i] for i in range(width // LANES)], axis=1)

    dq_ref[at, over] = unrotated(joined(dq) * factor)
    dk_ref[at, over] = unrotated(joined(dk) * factor)
    dv_ref[at, over] = joined(dv).astype(BF16)


def fused_kernel(
    n,
    replicas,
    m_hbm,
    o_ref,
    p_hbm,
    w_hbm,
    q_hbm,
    k_hbm,
    v_hbm,
    g_hbm,
    pos_ref,
    freq_ref,
    h_hbm,
    wg_hbm,
    dq_hbm,
    dk_hbm,
    dv_hbm,
    mall,
    owners,
    pre,
    slope,
    pre_send,
    pre_got,
    fall,
    w_ref,
    code,
    slotted,
    hid,
    linear_ref,
    hid_out,
    hid_got,
    h_ref,
    full,
    part,
    core_got,
    x_got,
    wg_ref,
    q_ref,
    k_ref,
    v_ref,
    g_ref,
    dq_ref,
    dk_ref,
    dv_ref,
    c_ref,
    s_ref,
    m_recv,
    up_sem,
    down_sem,
    side_sem,
    o_send,
    o_recv,
    p_send,
    p_recv,
    f_recv,
    mirror_sem,
    fup_sem,
    fdown_sem,
    fside_sem,
    fx_sem,
    fcore_sem,
    h_send,
    h_recv,
    c_send,
    c_recv,
    x_send,
    x_recv,
    local_sem,
    out_sem,
):
    line = n // SIDES
    near = n // 2
    near_line = line // 2
    rows_here, width = m_hbm.shape
    slots, units = pre.shape
    mine = units // n
    parts = w_hbm.shape[0]
    shared = parts > 1
    block = SIDES * rows_here
    patches, features = q_ref.shape
    chips = replicas // 2
    me = lax.axis_index("ctx")
    rep = lax.axis_index("dp")
    a, b = me // SIDES, me % SIDES
    side, row = a // near_line, a % near_line
    here = me % near
    mirror = (me + near) % n
    partner = rep // 2 * 2 + 1 - rep % 2
    core = rep % 2
    q_own = rep if shared else 0
    q_far = (rep + 2) % replicas if shared else 0

    barrier = pltpu.get_barrier_semaphore()
    for r in range(1, n):
        pl.semaphore_signal(barrier, inc=1, device_id={"dp": rep, "ctx": (me + r) % n}, device_id_type=MESH)
    pl.semaphore_signal(barrier, inc=1, device_id={"dp": partner, "ctx": me}, device_id_type=MESH)
    for r in range(1, chips):
        pl.semaphore_signal(
            barrier, inc=1, device_id={"dp": (rep + 2 * r) % replicas, "ctx": me}, device_id_type=MESH
        )
    locals_ = [
        pltpu.make_async_copy(p_hbm, pre, local_sem.at[0]),
        pltpu.make_async_copy(q_hbm, q_ref, local_sem.at[1]),
        pltpu.make_async_copy(k_hbm, k_ref, local_sem.at[2]),
        pltpu.make_async_copy(v_hbm, v_ref, local_sem.at[3]),
        pltpu.make_async_copy(g_hbm, g_ref, local_sem.at[4]),
        pltpu.make_async_copy(m_hbm, mall.at[me], local_sem.at[5]),
        pltpu.make_async_copy(w_hbm, w_ref, local_sem.at[6]),
        pltpu.make_async_copy(o_ref, owners.at[me], local_sem.at[7]),
    ]
    for copy in locals_:
        copy.start()
    pl.semaphore_wait(barrier, n - 1 + chips)

    def send(src, dst, send_sem, recv_sem, ctx=None, dp=None):
        where = {"dp": rep if dp is None else dp, "ctx": me if ctx is None else ctx}
        return pltpu.make_async_remote_copy(
            src_ref=src,
            dst_ref=dst,
            send_sem=send_sem,
            recv_sem=recv_sem,
            device_id=where,
            device_id_type=MESH,
        )

    def owner_copy(r):
        return send(o_ref, owners.at[me], o_send.at[r - 1], o_recv.at[r - 1], ctx=(me + r) % n)

    def unit_rows(peer):
        return pre_send.at[pl.ds(pl.multiple_of(peer * mine, 16), mine), :]

    def pre_place():
        return pre_got.at[:, pl.ds(pl.multiple_of(me * slots, LANES), slots)]

    def pre_copy(r):
        peer = (me + r) % n
        return send(unit_rows(peer), pre_place(), p_send.at[r - 1], p_recv.at[r - 1], ctx=peer)

    def hidden_copy(r):
        to = (here + r) % near
        return send(
            hid_out.at[to], hid_got.at[here], h_send.at[r - 1], h_recv.at[r - 1], ctx=side * near + to
        )

    def up_copy(t, ref):
        at = (a - t) * SIDES + b
        return send(ref, mall.at[at], up_sem.at[t], m_recv.at[at], ctx=me + SIDES)

    def down_copy(t, ref):
        at = (a + t) * SIDES + b
        return send(ref, mall.at[at], down_sem.at[t], m_recv.at[at], ctx=me - SIDES)

    def side_copy(at, ref):
        src = at * SIDES + b
        return send(ref, mall.at[src], side_sem.at[at], m_recv.at[src], ctx=a * SIDES + 1 - b)

    def m_arrived(src):
        send(mall.at[src], mall.at[src], up_sem.at[0], m_recv.at[src], ctx=a * SIDES + 1 - b).wait_recv()

    def mirror_copy():
        return send(
            w_hbm.at[q_own], fall.at[here, q_own], mirror_sem.at[0], f_recv.at[here, q_own], ctx=mirror
        )

    def fup_copy(t):
        at = (row - t) * SIDES + b
        ref = fall.at[at, q_own]
        return send(ref, ref, fup_sem.at[t], f_recv.at[at, q_own], ctx=me + SIDES)

    def fdown_copy(t):
        at = (row + t) * SIDES + b
        ref = fall.at[at, q_own]
        return send(ref, ref, fdown_sem.at[t], f_recv.at[at, q_own], ctx=me - SIDES)

    def fside_copy(at):
        src = at * SIDES + b
        ref = fall.at[src, q_own]
        return send(ref, ref, fside_sem.at[at], f_recv.at[src, q_own], ctx=a * SIDES + 1 - b)

    def fx_copy(src):
        ref = fall.at[src, q_own]
        return send(ref, ref, fx_sem.at[src], f_recv.at[src, q_own], dp=q_far)

    def fcore_copy(src, which):
        at = (q_own, q_far)[which]
        ref = fall.at[src, at]
        return send(ref, ref, fcore_sem.at[src, which], f_recv.at[src, at], dp=partner)

    def f_arrived(src, at):
        ref = fall.at[src, at]
        send(ref, ref, fup_sem.at[0], f_recv.at[src, at], ctx=a * SIDES + 1 - b).wait_recv()

    def core_copy(x):
        return send(
            part.at[2 * x + 1 - core], core_got.at[x], c_send.at[x], c_recv.at[x], dp=partner
        )

    def x_copy(r):
        peer = (rep + 2 * r) % replicas
        return send(part.at[peer], x_got.at[r - 1], x_send.at[r - 1], x_recv.at[r - 1], dp=peer)

    def when(condition, body):
        pl.when(condition)(body)

    for r in range(1, n):
        owner_copy(r).start()
    when(a + 1 < line, lambda: up_copy(0, m_hbm).start())
    when(a > 0, lambda: down_copy(0, m_hbm).start())
    side_copy(a, m_hbm).start()
    mirror_copy().start()

    locals_[0].wait()

    def turn(j, carry):
        over = pl.ds(pl.multiple_of(j * LANES, LANES), LANES)
        pre_send[over, :] = jnp.transpose(pre[:, over].astype(F32)).astype(BF16)
        return carry

    lax.fori_loop(0, units // LANES, turn, 0)
    own_pre = pltpu.make_async_copy(unit_rows(me), pre_place(), local_sem.at[8])
    own_pre.start()
    rope_tables(pos_ref, freq_ref, c_ref, s_ref)
    full[...] = jnp.zeros_like(full)
    slotted[...] = jnp.zeros_like(slotted)
    for copy in locals_[1:5]:
        copy.wait()

    def both(t, at, count, body):
        if t == 0:
            body(at, None)
        else:
            when(at - t >= 0, lambda: body(at - t, True))
            when(at + t < count, lambda: body(at + t, False))

    def send_pre():
        for r in range(1, n):
            pre_copy(r).start()

    def token_event(t):
        def body(at, below):
            src = at * SIDES + b
            ref = mall.at[src]
            m_arrived(src)
            if below:
                when(a + 1 < line, lambda: up_copy(t, ref).start())
            else:
                when(a > 0, lambda: down_copy(t, ref).start())
            side_copy(at, ref).start()

        both(t, a, line, body)

    def across(src):
        if shared:
            fx_copy(src).start()
            fcore_copy(src, 0).start()

    def weight_event(t):
        def body(at, below):
            src = at * SIDES + b
            f_arrived(src, q_own)
            if below is not False:
                when(row + 1 < near_line, lambda: fup_copy(t).start())
            if below is not True:
                when(row > 0, lambda: fdown_copy(t).start())
            across(src)

        both(t, row, near_line, body)

    def weight_turn(t):
        both(t, row, near_line, lambda at, below: fside_copy(at).start())

    def weight_side_event(t):
        def body(at, below):
            src = at * SIDES + 1 - b
            f_arrived(src, q_own)
            across(src)

        both(t, row, near_line, body)

    def weight_far_event(t, other):
        def body(at, below):
            src = at * SIDES + (1 - b if other else b)
            if shared:
                f_arrived(src, q_far)
                fcore_copy(src, 1).start()

        both(t, row, near_line, body)

    def event(kind, *given):
        return functools.partial(kind, *given)

    order = [
        (1, event(token_event, 1)),
        (2, event(weight_event, 0)),
        (2, event(weight_turn, 0)),
        (4, event(token_event, 2)),
        (4, send_pre),
        (5, event(weight_side_event, 0)),
        (6, event(weight_event, 1)),
        (6, event(weight_turn, 1)),
        (6, event(weight_far_event, 0, False)),
    ]

    halves = 2
    span = features // halves
    steps = patches // WIN * halves

    def attend(i, carry):
        at = pl.ds(pl.multiple_of(i // halves * WIN, WIN), WIN)
        over = pl.ds(pl.multiple_of(i % halves * span, LANES), span)
        attention_part(
            at, over, (q_ref, k_ref, v_ref, g_ref), c_ref, s_ref, (dq_ref, dk_ref, dv_ref)
        )
        for step in range(steps):
            todo = [run for index, run in order if index == step]
            if todo:
                when(i == step, lambda todo=todo: [run() for run in todo] and None)
        return carry

    lax.fori_loop(0, steps, attend, 0)
    outs = [
        pltpu.make_async_copy(dq_ref, dq_hbm, out_sem.at[0]),
        pltpu.make_async_copy(dk_ref, dk_hbm, out_sem.at[1]),
        pltpu.make_async_copy(dv_ref, dv_hbm, out_sem.at[2]),
    ]
    for copy in outs:
        copy.start()

    far = (1 - side) * (units // 2)

    def incline(j, carry):
        x = pre[:, pl.ds(pl.multiple_of(far + j * LANES, LANES), LANES)].astype(F32)
        cdf = 0.5 * (1.0 + lax.erf(x * 0.5**0.5))
        slope[:, pl.ds(pl.multiple_of(j * LANES, LANES), LANES)] = cdf + x * jnp.exp(-0.5 * x * x) * (
            2.0 * math.pi
        ) ** (-0.5)
        return carry

    lax.fori_loop(0, units // 2 // LANES, incline, 0)

    for copy in locals_[5:]:
        copy.wait()
    for r in range(1, n):
        owner_copy(r).wait()
    padded = -(-n // 16) * 16
    earlier = lax.broadcasted_iota(jnp.int32, (rows_here, rows_here), 0) < lax.broadcasted_iota(
        jnp.int32, (rows_here, rows_here), 1
    )
    earlier = earlier.astype(F32).astype(BF16)
    names = lax.broadcasted_iota(jnp.int32, (padded, rows_here), 0)
    base = jnp.zeros((padded, 1), F32)
    for s in range(n):
        onehot = (names == owners[s]).astype(F32)
        count = dot(onehot.astype(BF16), earlier) + base
        position = jnp.sum(onehot * (count + names.astype(F32) * float(slots)), axis=0, keepdims=True)
        base = base + jnp.sum(onehot, axis=1, keepdims=True)
        lo = s % SIDES * rows_here
        code[s // SIDES, :, lo : lo + rows_here] = jnp.broadcast_to(position, (8, rows_here))
    standing = lax.broadcasted_iota(jnp.int32, (slots, block), 0).astype(F32)

    def landing(o, t):
        first = (o * slots).astype(F32)
        return (standing == code[t, 0:1, :] - first).astype(F32).astype(BF16)

    def nth(d):
        low = jnp.where(d <= a, a - d, d)
        flip = line - 1 - a
        high = line - 1 - jnp.where(d <= flip, flip - d, d)
        return jnp.where(side == 0, low, high)

    def gathered(t):
        return jnp.concatenate([mall[t * SIDES + i] for i in range(SIDES)], axis=0)

    def early(d, carry):
        t = nth(d)
        m_arrived(t * SIDES + 1 - b)
        rows = gathered(t)
        linear_ref[t] = dot(w_ref[...].reshape(mine, width), rows, NT)
        slotted[...] += dot(landing(me, t), rows).astype(BF16)
        return carry


    def late(d, carry):
        t = nth(d)

        spots = jnp.concatenate([landing(jnp.int32(o), t) for o in range(n)], axis=0)
        x = dot(pre_got[...], spots)
        cdf = 0.5 * (1.0 + lax.erf(x * 0.5**0.5))
        incline = cdf + x * jnp.exp(-0.5 * x * x) * (2.0 * math.pi) ** (-0.5)
        hid[:, pl.ds(pl.multiple_of(t * block, LANES), block)] = (linear_ref[t] * incline).astype(BF16)
        full[...] += dot((x * cdf).astype(BF16), gathered(t))
        return carry

    lax.fori_loop(0, line - 1, early, 0)
    for t in range(2, near_line):
        weight_event(t)
        weight_turn(t)
    weight_far_event(0, True)
    for t in range(1, near_line):
        weight_far_event(t, False)
    for t in range(3, line):
        token_event(t)
    for r in range(1, n):
        pre_copy(r).wait()
    own_pre.wait()
    lax.fori_loop(0, line - 1, late, 0)
    for t in range(1, near_line):
        weight_side_event(t)
    early(line - 1, 0)
    late(line - 1, 0)


    piece = width // replicas
    for d in range(replicas):
        lo = d * piece // LANES * LANES
        hi = -(-(d + 1) * piece // LANES) * LANES
        shift = d * piece - lo
        value = full[:, lo:hi]
        if shift:
            value = pltpu.roll(value, hi - lo - shift, 1)
        part[d] = value[:, :piece]
    for x in range(chips):
        core_copy(x).start()

    def outgoing(i, carry):
        spots = jnp.concatenate([landing(side * near + i, t) for t in range(line)], axis=1)
        hid_out[i] = dot(hid[...], spots, NT).astype(BF16)
        return carry

    lax.fori_loop(0, near, outgoing, 0)
    for r in range(1, near):
        hidden_copy(r).start()
    own_hidden = pltpu.make_async_copy(hid_out.at[here], hid_got.at[here], local_sem.at[9])
    own_hidden.start()

    for x in range(chips):
        core_copy(x).wait()
    for x in range(chips):
        part[2 * x + core] = part[2 * x + core] + core_got[x]
    for r in range(1, chips):
        x_copy(r).start()

    groups = next(g for g in range(near_line, 0, -1) if near_line % g == 0 and units // 2 // g % LANES == 0)
    run, each = near // groups, units // 2 // groups

    def linear(g, carry):
        if shared:

            def await_rest(i, carry):
                for other in (partner, (partner + 2) % replicas):
                    f_arrived(g * run + i, other)
                return carry

            lax.fori_loop(0, run, await_rest, 0)
        weight = fall[pl.ds(g * run, run)].reshape(each, width)
        over = pl.ds(pl.multiple_of(g * each, LANES), each)
        to = pl.ds(pl.multiple_of(far + g * each, LANES), each)
        h_ref[:, to] = (dot(slotted[...], weight, NT) * slope[:, over]).astype(BF16)
        return carry

    for t in range(1, near_line):
        weight_far_event(t, True)
    lax.fori_loop(0, groups, linear, 0)

    own_hidden.wait()
    for r in range(1, near):
        hidden_copy(r).wait()
    spot = lax.broadcasted_iota(jnp.int32, (slots, slots), 0) == lax.broadcasted_iota(
        jnp.int32, (slots, slots), 1
    )
    spot = spot.astype(F32).astype(BF16)

    def settle(g, carry):
        rows = hid_got[pl.ds(g * run, run)].reshape(each, slots)
        to = pl.ds(pl.multiple_of(side * (units // 2) + g * each, LANES), each)
        h_ref[:, to] = dot(spot, rows, NT).astype(BF16)
        return carry

    lax.fori_loop(0, groups, settle, 0)
    outs.append(pltpu.make_async_copy(h_ref, h_hbm, out_sem.at[3]))
    outs[-1].start()

    total = part[rep]
    for r in range(1, chips):
        x_copy(r).wait()
        total = total + x_got[r - 1]
    wg_ref[...] = total * (rows_here * n * replicas) ** (-0.5)
    outs.append(pltpu.make_async_copy(wg_ref, wg_hbm, out_sem.at[4]))
    outs[-1].start()

    def sent(t, carry):
        @pl.when((a - t >= 0) & (a + 1 < line))
        def _():
            up_copy(t, mall.at[me]).wait_send()

        @pl.when((a + t < line) & (a > 0))
        def _():
            down_copy(t, mall.at[me]).wait_send()

        side_copy(t, mall.at[me]).wait_send()
        return carry

    lax.fori_loop(0, line, sent, 0)
    mirror_copy().wait_send()

    def weight_sent(t, carry):
        @pl.when((row - t >= 0) & (row + 1 < near_line))
        def _():
            fup_copy(t).wait_send()

        @pl.when((row + t < near_line) & (row > 0))
        def _():
            fdown_copy(t).wait_send()

        fside_copy(t).wait_send()
        return carry

    lax.fori_loop(0, near_line, weight_sent, 0)
    if shared:

        def passed(src, carry):
            fx_copy(src).wait_send()
            fcore_copy(src, 0).wait_send()
            fcore_copy(src, 1).wait_send()
            return carry

        lax.fori_loop(0, near, passed, 0)
    for copy in outs:
        copy.wait()


def finish_kernel(*refs):
    ins, outs, held = refs[:5], refs[5:10], refs[10:15]
    in_sem, out_sem = refs[15:]
    first = [pltpu.make_async_copy(ins[i], held[i], in_sem.at[i]) for i in range(5)]
    second = [pltpu.make_async_copy(held[i], outs[i], out_sem.at[i]) for i in range(5)]
    for copy in first:
        copy.start()
    for i in range(5):
        first[i].wait()
        second[i].start()
    for copy in second:
        copy.wait()


def fused(merged_grad, merged_owner, merger_pre, fc2_weight, query, key_states, value_states, out_grad, position):
    rows_here, width = merged_grad.shape
    n, replicas = lax.axis_size("ctx"), lax.axis_size("dp")
    slots, units = merger_pre.shape
    mine = units // n
    line = n // SIDES
    near = n // 2
    near_line = line // 2
    block = SIDES * rows_here
    piece = width // replicas
    chips = replicas // 2
    parts = replicas if chips == 2 and mine % (16 * replicas) == 0 else 1
    quarter = HEAD // 4
    freq = 1.0 / 10000.0 ** (jnp.arange(quarter, dtype=F32) * (4.0 / HEAD))
    freq = jnp.concatenate([freq] * 4 + [jnp.zeros((LANES - HEAD,), F32)]).reshape(1, LANES)
    vmem = pl.BlockSpec(memory_space=pltpu.VMEM)
    hbm = pl.BlockSpec(memory_space=pl.ANY)
    dma = pltpu.SemaphoreType.DMA
    like = jax.ShapeDtypeStruct(query.shape, BF16)
    shapes = [
        jax.ShapeDtypeStruct((slots, units), BF16),
        jax.ShapeDtypeStruct((mine, piece), F32),
        like,
        like,
        like,
    ]
    results = pl.pallas_call(
        functools.partial(fused_kernel, n, replicas),
        in_specs=[hbm, vmem] + [hbm] * 6 + [vmem] * 2,
        out_specs=[hbm] * 5,
        out_shape=shapes,
        scratch_shapes=[
            pltpu.VMEM((n, rows_here, width), BF16),
            pltpu.VMEM((n, 1, rows_here), jnp.int32),
            pltpu.VMEM((slots, units), BF16),
            pltpu.VMEM((slots, units // 2), F32),
            pltpu.VMEM((units, slots), BF16),
            pltpu.VMEM((mine, n * slots), BF16),
            pltpu.VMEM((near, parts, mine // parts, width), BF16),
            pltpu.VMEM((parts, mine // parts, width), BF16),
            pltpu.VMEM((line, 8, block), F32),
            pltpu.VMEM((slots, width), BF16),
            pltpu.VMEM((mine, line * block), BF16),
            pltpu.VMEM((line, mine, block), F32),
            pltpu.VMEM((near, mine, slots), BF16),
            pltpu.VMEM((near, mine, slots), BF16),
            pltpu.VMEM((slots, units), BF16),
            pltpu.VMEM((mine, width), F32),
            pltpu.VMEM((replicas, mine, piece), F32),
            pltpu.VMEM((chips, mine, piece), F32),
            pltpu.VMEM((max(chips - 1, 1), mine, piece), F32),
            pltpu.VMEM((mine, piece), F32),
        ]
        + [pltpu.VMEM(query.shape, BF16)] * 7
        + [
            pltpu.VMEM((query.shape[0], LANES), F32),
            pltpu.VMEM((query.shape[0], LANES), F32),
            dma((n,)),
            dma((line,)),
            dma((line,)),
            dma((line,)),
            dma((n - 1,)),
            dma((n - 1,)),
            dma((n - 1,)),
            dma((n - 1,)),
            dma((near, parts)),
            dma((1,)),
            dma((near_line,)),
            dma((near_line,)),
            dma((near_line,)),
            dma((near,)),
            dma((near, 2)),
            dma((near - 1,)),
            dma((near - 1,)),
            dma((chips,)),
            dma((chips,)),
            dma((max(chips - 1, 1),)),
            dma((max(chips - 1, 1),)),
            dma((10,)),
            dma((5,)),
        ],
        compiler_params=pltpu.CompilerParams(
            collective_id=0, has_side_effects=True, vmem_limit_bytes=60 * 2**20
        ),
        name="fused",
    )(
        merged_grad,
        merged_owner.reshape(1, rows_here),
        merger_pre,
        fc2_weight.reshape(parts, mine // parts, width),
        query,
        key_states,
        value_states,
        out_grad,
        position,
        freq,
    )
    return tuple(
        pl.pallas_call(
            finish_kernel,
            in_specs=[hbm] * 5,
            out_specs=[hbm] * 5,
            out_shape=shapes,
            scratch_shapes=[pltpu.VMEM(shape.shape, shape.dtype) for shape in shapes] + [dma((5,)), dma((5,))],
            name="finish",
        )(*results)
    )


def solution(mesh):
    every = P(("dp", "ctx"), None)
    return jax.shard_map(
        fused,
        mesh=mesh,
        in_specs=(every, every, every, P("ctx", None)) + (every,) * 4 + (P(None, ("dp", "ctx")),),
        out_specs=(every, P("ctx", "dp")) + (every,) * 3,
        check_vma=False,
    )
```

```python
import functools
import math

import jax
import jax.numpy as jnp
from jax import lax
from jax.experimental import pallas as pl
from jax.experimental.pallas import tpu as pltpu
from jax.sharding import PartitionSpec as P

HEAD = 80
WIN = 64
LANES = 128
SIDES = 2
CUTS = 2
F32 = jnp.float32
BF16 = jnp.bfloat16
MESH = pl.DeviceIdType.MESH
NT = (((1,), (1,)), ((), ()))
TN = (((0,), (0,)), ((), ()))
NN = (((1,), (0,)), ((), ()))


def dot(a, b, dims=NN):
    return lax.dot_general(a, b, dims, preferred_element_type=F32)


def spread(table, width):
    shape = (LANES, width)
    lane = lax.broadcasted_iota(jnp.int32, shape, 1) % HEAD
    pick = (lane == lax.broadcasted_iota(jnp.int32, shape, 0)).astype(F32).astype(BF16)
    high = table.astype(BF16)
    rest = table - high.astype(F32)
    mid = rest.astype(BF16)
    low = (rest - mid.astype(F32)).astype(BF16)
    return dot(high, pick) + dot(mid, pick) + dot(low, pick)


def rope_tables(pos_ref, c_ref, s_ref):
    count = pos_ref.shape[1]
    half, quarter = HEAD // 2, HEAD // 4
    unit = lax.broadcasted_iota(jnp.int32, (LANES, count), 0)
    rows = pos_ref[0:1, :].astype(F32)
    cols = pos_ref[1:2, :].astype(F32)
    rank = (unit % half % quarter).astype(F32)
    freq = jnp.exp(rank * (-4.0 / HEAD * math.log(10000.0)))
    angles = jnp.where(unit % half < quarter, rows, cols) * freq
    c_ref[...] = jnp.transpose(jnp.cos(angles))
    s_ref[...] = jnp.transpose(jnp.where(unit < half, -1.0, 1.0) * jnp.sin(angles))


def attention_part(at, over, refs, c_ref, s_ref, outs):
    q_ref, k_ref, v_ref, g_ref = refs
    dq_ref, dk_ref, dv_ref = outs
    width = over.size
    heads = width // HEAD
    half = HEAD // 2
    cosine = spread(c_ref[at, :], width)
    sine = spread(s_ref[at, :], width)
    lane = lax.broadcasted_iota(jnp.int32, (WIN, width), 1)
    first = lane % HEAD < half

    def swap(x):
        return jnp.where(first, pltpu.roll(x, width - half, 1), pltpu.roll(x, half, 1))

    def rotated(x):
        return (x * cosine + swap(x) * sine).astype(BF16)

    def unrotated(x):
        return (x * cosine - swap(x) * sine).astype(BF16)

    q = rotated(q_ref[at, over].astype(F32))
    k = rotated(k_ref[at, over].astype(F32))
    v = v_ref[at, over]
    g = g_ref[at, over]
    factor = HEAD ** (-0.5)
    dq, dk, dv = {}, {}, {}

    def add(into, tile, value):
        for i in range(value.shape[1] // LANES):
            part = value[:, i * LANES : (i + 1) * LANES]
            into[tile + i] = into[tile + i] + part if tile + i in into else part

    for head in range(heads):
        tile = head * HEAD // LANES
        end = -(-(head + 1) * HEAD // LANES)
        lo, hi = tile * LANES, end * LANES
        here = lax.broadcasted_iota(jnp.int32, (1, hi - lo), 1) + lo
        mask = ((here >= head * HEAD) & (here < (head + 1) * HEAD)).astype(F32).astype(BF16)
        qm = q[:, lo:hi] * mask
        km = k[:, lo:hi] * mask
        gm = g[:, lo:hi] * mask
        scores = dot(qm, k[:, lo:hi], NT) * factor
        weight = jnp.exp(scores - jnp.max(scores, axis=1, keepdims=True))
        probs = weight * (1.0 / jnp.sum(weight, axis=1, keepdims=True))
        probs_b = probs.astype(BF16)
        prob_grad = dot(gm, v[:, lo:hi], NT)
        delta = jnp.sum(probs_b.astype(F32) * prob_grad, axis=1, keepdims=True)
        score_grad = (probs * (prob_grad - delta)).astype(BF16)
        add(dv, tile, dot(probs_b, gm, TN))
        add(dq, tile, dot(score_grad, km, NN))
        add(dk, tile, dot(score_grad, qm, TN))

    def joined(parts):
        return jnp.concatenate([parts[i] for i in range(width // LANES)], axis=1)

    dq_ref[at, over] = unrotated(joined(dq) * factor)
    dk_ref[at, over] = unrotated(joined(dk) * factor)
    dv_ref[at, over] = joined(dv).astype(BF16)


def fused_kernel(
    n,
    replicas,
    m_hbm,
    o_ref,
    p_hbm,
    w_hbm,
    q_hbm,
    k_hbm,
    v_hbm,
    g_hbm,
    pos_ref,
    h_hbm,
    wg_hbm,
    dq_hbm,
    dk_hbm,
    dv_hbm,
    mall,
    owners,
    pre,
    slope,
    pre_send,
    pre_got,
    fall,
    w_ref,
    code,
    slotted,
    hid,
    linear_ref,
    act_ref,
    hid_out,
    hid_got,
    h_ref,
    full,
    part,
    core_got,
    x_out,
    x_got,
    wg_ref,
    q_ref,
    k_ref,
    v_ref,
    g_ref,
    dq_ref,
    dk_ref,
    dv_ref,
    c_ref,
    s_ref,
    m_recv,
    up_sem,
    down_sem,
    side_sem,
    o_send,
    o_recv,
    p_send,
    p_recv,
    f_recv,
    mirror_sem,
    fup_sem,
    fdown_sem,
    fside_sem,
    fx_sem,
    fcore_sem,
    h_send,
    h_recv,
    c_send,
    c_recv,
    x_send,
    x_recv,
    local_sem,
    out_sem,
):
    line = n // SIDES
    near = n // 2
    near_line = line // 2
    rows_here, width = m_hbm.shape
    slots, units = pre.shape
    mine = units // n
    parts = w_hbm.shape[0]
    shared = parts > 1
    block = SIDES * rows_here
    patches, features = q_ref.shape
    chips = replicas // 2
    me = lax.axis_index("ctx")
    rep = lax.axis_index("dp")
    a, b = me // SIDES, me % SIDES
    side, row = a // near_line, a % near_line
    here = me % near
    mirror = (me + near) % n
    partner = rep // 2 * 2 + 1 - rep % 2
    core, place = rep % 2, rep // 2
    q_own = rep if shared else 0
    q_far = (rep + 2) % replicas if shared else 0

    barrier = pltpu.get_barrier_semaphore()
    for r in range(1, n):
        pl.semaphore_signal(barrier, inc=1, device_id={"dp": rep, "ctx": (me + r) % n}, device_id_type=MESH)
    pl.semaphore_signal(barrier, inc=1, device_id={"dp": partner, "ctx": me}, device_id_type=MESH)
    for r in range(1, chips):
        pl.semaphore_signal(
            barrier, inc=1, device_id={"dp": (rep + 2 * r) % replicas, "ctx": me}, device_id_type=MESH
        )
    locals_ = [
        pltpu.make_async_copy(p_hbm, pre, local_sem.at[0]),
        pltpu.make_async_copy(q_hbm, q_ref, local_sem.at[1]),
        pltpu.make_async_copy(k_hbm, k_ref, local_sem.at[2]),
        pltpu.make_async_copy(v_hbm, v_ref, local_sem.at[3]),
        pltpu.make_async_copy(g_hbm, g_ref, local_sem.at[4]),
        pltpu.make_async_copy(m_hbm, mall.at[me], local_sem.at[5]),
        pltpu.make_async_copy(w_hbm, w_ref, local_sem.at[6]),
        pltpu.make_async_copy(o_ref, owners.at[me], local_sem.at[7]),
    ]
    for copy in locals_:
        copy.start()
    pl.semaphore_wait(barrier, n - 1 + chips)

    def send(src, dst, send_sem, recv_sem, ctx=None, dp=None):
        where = {"dp": rep if dp is None else dp, "ctx": me if ctx is None else ctx}
        return pltpu.make_async_remote_copy(
            src_ref=src,
            dst_ref=dst,
            send_sem=send_sem,
            recv_sem=recv_sem,
            device_id=where,
            device_id_type=MESH,
        )

    def owner_copy(r):
        return send(o_ref, owners.at[me], o_send.at[r - 1], o_recv.at[r - 1], ctx=(me + r) % n)

    def unit_rows(peer):
        return pre_send.at[pl.ds(pl.multiple_of(peer * mine, 16), mine), :]

    def pre_place():
        return pre_got.at[:, pl.ds(pl.multiple_of(me * slots, LANES), slots)]

    def pre_copy(r):
        peer = (me + r) % n
        return send(unit_rows(peer), pre_place(), p_send.at[r - 1], p_recv.at[r - 1], ctx=peer)

    def hidden_copy(r):
        to = (here + r) % near
        return send(
            hid_out.at[to], hid_got.at[here], h_send.at[r - 1], h_recv.at[r - 1], ctx=side * near + to
        )

    def cut(h):
        return pl.ds(h * (rows_here // CUTS), rows_here // CUTS)

    def up_copy(t, ref, h):
        at = (a - t) * SIDES + b
        return send(ref.at[cut(h)], mall.at[at, cut(h)], up_sem.at[t, h], m_recv.at[at, h], ctx=me + SIDES)

    def down_copy(t, ref, h):
        at = (a + t) * SIDES + b
        return send(ref.at[cut(h)], mall.at[at, cut(h)], down_sem.at[t, h], m_recv.at[at, h], ctx=me - SIDES)

    def side_copy(at, ref, h):
        src = at * SIDES + b
        to = a * SIDES + 1 - b
        return send(ref.at[cut(h)], mall.at[src, cut(h)], side_sem.at[at, h], m_recv.at[src, h], ctx=to)

    def m_arrived(src, h):
        ref = mall.at[src, cut(h)]
        send(ref, ref, up_sem.at[0, 0], m_recv.at[src, h], ctx=a * SIDES + 1 - b).wait_recv()

    def mirror_copy():
        return send(
            w_hbm.at[q_own], fall.at[here, q_own], mirror_sem.at[0], f_recv.at[here, q_own], ctx=mirror
        )

    def fup_copy(t):
        at = (row - t) * SIDES + b
        ref = fall.at[at, q_own]
        return send(ref, ref, fup_sem.at[t], f_recv.at[at, q_own], ctx=me + SIDES)

    def fdown_copy(t):
        at = (row + t) * SIDES + b
        ref = fall.at[at, q_own]
        return send(ref, ref, fdown_sem.at[t], f_recv.at[at, q_own], ctx=me - SIDES)

    def fside_copy(at):
        src = at * SIDES + b
        ref = fall.at[src, q_own]
        return send(ref, ref, fside_sem.at[at], f_recv.at[src, q_own], ctx=a * SIDES + 1 - b)

    def fx_copy(src):
        ref = fall.at[src, q_own]
        return send(ref, ref, fx_sem.at[src], f_recv.at[src, q_own], dp=q_far)

    def fcore_copy(src, which):
        at = (q_own, q_far)[which]
        ref = fall.at[src, at]
        return send(ref, ref, fcore_sem.at[src, which], f_recv.at[src, at], dp=partner)

    def f_arrived(src, at):
        ref = fall.at[src, at]
        send(ref, ref, fup_sem.at[0], f_recv.at[src, at], ctx=a * SIDES + 1 - b).wait_recv()

    def core_copy(x):
        return send(
            part.at[2 * x + 1 - core], core_got.at[x], c_send.at[x], c_recv.at[x], dp=partner
        )

    def x_copy(r):
        peer = (rep + 2 * r) % replicas
        return send(x_out.at[r - 1], x_got.at[r - 1], x_send.at[r - 1], x_recv.at[r - 1], dp=peer)

    def when(condition, body):
        pl.when(condition)(body)

    for r in range(1, n):
        owner_copy(r).start()
    for h in range(CUTS):
        when(a + 1 < line, lambda h=h: up_copy(0, m_hbm, h).start())
        when(a > 0, lambda h=h: down_copy(0, m_hbm, h).start())
        side_copy(a, m_hbm, h).start()
    mirror_copy().start()

    locals_[0].wait()

    def turn(j, carry):
        over = pl.ds(pl.multiple_of(j * LANES, LANES), LANES)
        pre_send[over, :] = jnp.transpose(pre[:, over].astype(F32)).astype(BF16)
        return carry

    lax.fori_loop(0, units // LANES, turn, 0)
    own_pre = pltpu.make_async_copy(unit_rows(me), pre_place(), local_sem.at[8])
    own_pre.start()
    rope_tables(pos_ref, c_ref, s_ref)
    full[...] = jnp.zeros_like(full)
    slotted[...] = jnp.zeros_like(slotted)
    for copy in locals_[1:5]:
        copy.wait()

    def both(t, at, count, body):
        if t == 0:
            body(at, None)
        else:
            when(at - t >= 0, lambda: body(at - t, True))
            when(at + t < count, lambda: body(at + t, False))

    def send_pre():
        for r in range(1, n):
            pre_copy(r).start()

    def token_event(t):
        def body(at, below):
            src = at * SIDES + b
            ref = mall.at[src]
            for h in range(CUTS):
                m_arrived(src, h)
                if below:
                    when(a + 1 < line, lambda h=h: up_copy(t, ref, h).start())
                else:
                    when(a > 0, lambda h=h: down_copy(t, ref, h).start())
                side_copy(at, ref, h).start()

        both(t, a, line, body)

    def across(src):
        if shared:
            fx_copy(src).start()
            fcore_copy(src, 0).start()

    def weight_event(t):
        def body(at, below):
            src = at * SIDES + b
            f_arrived(src, q_own)
            if below is not False:
                when(row + 1 < near_line, lambda: fup_copy(t).start())
            if below is not True:
                when(row > 0, lambda: fdown_copy(t).start())
            across(src)

        both(t, row, near_line, body)

    def weight_turn(t):
        both(t, row, near_line, lambda at, below: fside_copy(at).start())

    def weight_side_event(t):
        def body(at, below):
            src = at * SIDES + 1 - b
            f_arrived(src, q_own)
            across(src)

        both(t, row, near_line, body)

    def weight_far_event(t, other):
        def body(at, below):
            src = at * SIDES + (1 - b if other else b)
            if shared:
                f_arrived(src, q_far)
                fcore_copy(src, 1).start()

        both(t, row, near_line, body)

    def event(kind, *given):
        return functools.partial(kind, *given)

    order = [
        (1, event(token_event, 1)),
        (2, event(weight_event, 0)),
        (2, event(weight_turn, 0)),
        (4, event(token_event, 2)),
        (4, send_pre),
        (5, event(weight_side_event, 0)),
        (6, event(weight_event, 1)),
        (6, event(weight_turn, 1)),
        (6, event(weight_far_event, 0, False)),
    ]

    halves = 2
    span = features // halves
    steps = patches // WIN * halves

    def attend(i, carry):
        at = pl.ds(pl.multiple_of(i // halves * WIN, WIN), WIN)
        over = pl.ds(pl.multiple_of(i % halves * span, LANES), span)
        attention_part(
            at, over, (q_ref, k_ref, v_ref, g_ref), c_ref, s_ref, (dq_ref, dk_ref, dv_ref)
        )
        for step in range(steps):
            todo = [run for index, run in order if index == step]
            if todo:
                when(i == step, lambda todo=todo: [run() for run in todo] and None)
        return carry

    lax.fori_loop(0, steps, attend, 0)
    outs = [
        pltpu.make_async_copy(dq_ref, dq_hbm, out_sem.at[0]),
        pltpu.make_async_copy(dk_ref, dk_hbm, out_sem.at[1]),
        pltpu.make_async_copy(dv_ref, dv_hbm, out_sem.at[2]),
    ]
    for copy in outs:
        copy.start()

    far = (1 - side) * (units // 2)

    def incline(j, carry):
        x = pre[:, pl.ds(pl.multiple_of(far + j * LANES, LANES), LANES)].astype(F32)
        cdf = 0.5 * (1.0 + lax.erf(x * 0.5**0.5))
        slope[:, pl.ds(pl.multiple_of(j * LANES, LANES), LANES)] = cdf + x * jnp.exp(-0.5 * x * x) * (
            2.0 * math.pi
        ) ** (-0.5)
        return carry

    lax.fori_loop(0, units // 2 // LANES, incline, 0)

    for copy in locals_[5:]:
        copy.wait()
    for r in range(1, n):
        owner_copy(r).wait()
    padded = -(-n // 16) * 16
    earlier = lax.broadcasted_iota(jnp.int32, (rows_here, rows_here), 0) < lax.broadcasted_iota(
        jnp.int32, (rows_here, rows_here), 1
    )
    earlier = earlier.astype(F32).astype(BF16)
    names = lax.broadcasted_iota(jnp.int32, (padded, rows_here), 0)
    base = jnp.zeros((padded, 1), F32)
    for s in range(n):
        onehot = (names == owners[s]).astype(F32)
        count = dot(onehot.astype(BF16), earlier) + base
        position = jnp.sum(onehot * (count + names.astype(F32) * float(slots)), axis=0, keepdims=True)
        base = base + jnp.sum(onehot, axis=1, keepdims=True)
        lo = s % SIDES * rows_here
        code[s // SIDES, :, lo : lo + rows_here] = jnp.broadcast_to(position, (8, rows_here))
    standing = lax.broadcasted_iota(jnp.int32, (slots, block), 0).astype(F32)

    def landing(o, t):
        first = (o * slots).astype(F32)
        return (standing == code[t, 0:1, :] - first).astype(F32).astype(BF16)

    def nth(d):
        low = jnp.where(d <= a, a - d, d)
        flip = line - 1 - a
        high = line - 1 - jnp.where(d <= flip, flip - d, d)
        return jnp.where(side == 0, low, high)

    def gathered(t):
        return jnp.concatenate([mall[t * SIDES + i] for i in range(SIDES)], axis=0)

    def slotting(t, rows):
        slotted[...] += dot(landing(me, t), rows).astype(BF16)

    def early(d, carry):
        t = nth(d)
        for h in range(CUTS):
            m_arrived(t * SIDES + 1 - b, h)
        rows = gathered(t)
        linear_ref[t] = dot(w_ref[...].reshape(mine, width), rows, NT)
        slotting(t, rows)
        return carry

    def activation(t):
        spots = jnp.concatenate([landing(jnp.int32(o), t) for o in range(n)], axis=0)
        x = dot(pre_got[...], spots)
        cdf = 0.5 * (1.0 + lax.erf(x * 0.5**0.5))
        incline = cdf + x * jnp.exp(-0.5 * x * x) * (2.0 * math.pi) ** (-0.5)
        return (x * cdf).astype(BF16), incline

    def hid_place(t):
        return pl.ds(pl.multiple_of(t * block, LANES), block)

    def late(d, carry):
        t = nth(d)
        act, incline = activation(t)
        hid[:, hid_place(t)] = (linear_ref[t] * incline).astype(BF16)
        full[...] += dot(act, gathered(t))
        return carry

    lax.fori_loop(0, line - 1, early, 0)
    for t in range(2, near_line):
        weight_event(t)
        weight_turn(t)
    weight_far_event(0, True)
    for t in range(1, near_line):
        weight_far_event(t, False)
    for t in range(3, line):
        token_event(t)
    for t in range(1, near_line):
        weight_side_event(t)
    for r in range(1, n):
        pre_copy(r).wait()
    own_pre.wait()
    lax.fori_loop(0, line - 1, late, 0)
    last = nth(jnp.int32(line - 1))
    act_ref[...], linear_ref[last] = activation(last)
    for h in range(CUTS):
        m_arrived(last * SIDES + 1 - b, h)
    full[...] += dot(act_ref[...], gathered(last))


    piece = width // replicas
    span_out = part.shape[2]
    for d in range(replicas):
        lo = d * piece // LANES * LANES
        hi = -(-(d + 1) * piece // LANES) * LANES
        shift = d * piece - lo
        value = full[:, lo:hi]
        if shift:
            value = pltpu.roll(value, hi - lo - shift, 1)
        part[d] = value[:, :span_out]
    for x in range(chips):
        core_copy(x).start()
    late_rows = gathered(last)
    late_linear = dot(w_ref[...].reshape(mine, width), late_rows, NT)
    hid[:, hid_place(last)] = (late_linear * linear_ref[last]).astype(BF16)

    tight = x_out.shape[1] < mine
    rest = piece % LANES
    whole = piece - rest
    lane = lax.broadcasted_iota(jnp.int32, (mine // 2, LANES), 1)

    def packed(value):
        if not tight:
            return value
        top, low = value[: mine // 2], value[mine // 2 :]
        low = pltpu.roll(low, rest, 1)
        seam = jnp.where(lane < rest, top[:, whole:], low[:, :LANES])
        return jnp.concatenate([top[:, :whole], seam, low[:, LANES:]], axis=1)

    def unpacked(value):
        if not tight:
            return value
        low = pltpu.roll(value[:, whole:], span_out - rest, 1)
        return jnp.concatenate([value[:, :span_out], low], axis=0)

    for x in range(chips):
        core_copy(x).wait()
    for r in range(1, chips):
        x = (place + r) % chips
        x_out[r - 1] = packed(part[2 * x + core] + core_got[x]).astype(x_out.dtype)
        x_copy(r).start()

    def outgoing(i, carry):
        spots = jnp.concatenate([landing(side * near + i, t) for t in range(line)], axis=1)
        hid_out[i] = dot(hid[...], spots, NT).astype(BF16)
        return carry

    lax.fori_loop(0, near, outgoing, 0)
    for r in range(1, near):
        hidden_copy(r).start()
    own_hidden = pltpu.make_async_copy(hid_out.at[here], hid_got.at[here], local_sem.at[9])
    own_hidden.start()


    groups = next(g for g in range(near_line, 0, -1) if near_line % g == 0 and units // 2 // g % LANES == 0)
    run, each = near // groups, units // 2 // groups

    def linear(g, carry):
        if shared:

            def await_rest(i, carry):
                for other in (partner, (partner + 2) % replicas):
                    f_arrived(g * run + i, other)
                return carry

            lax.fori_loop(0, run, await_rest, 0)
        weight = fall[pl.ds(g * run, run)].reshape(each, width)
        over = pl.ds(pl.multiple_of(g * each, LANES), each)
        to = pl.ds(pl.multiple_of(far + g * each, LANES), each)
        h_ref[:, to] = (dot(slotted[...], weight, NT) * slope[:, over]).astype(BF16)
        return carry

    slotting(last, gathered(last))
    for t in range(1, near_line):
        weight_far_event(t, True)
    lax.fori_loop(0, groups, linear, 0)

    own_hidden.wait()
    for r in range(1, near):
        hidden_copy(r).wait()
    spot = lax.broadcasted_iota(jnp.int32, (slots, slots), 0) == lax.broadcasted_iota(
        jnp.int32, (slots, slots), 1
    )
    spot = spot.astype(F32).astype(BF16)

    def settle(g, carry):
        rows = hid_got[pl.ds(g * run, run)].reshape(each, slots)
        to = pl.ds(pl.multiple_of(side * (units // 2) + g * each, LANES), each)
        h_ref[:, to] = dot(spot, rows, NT).astype(BF16)
        return carry

    lax.fori_loop(0, groups, settle, 0)
    outs.append(pltpu.make_async_copy(h_ref, h_hbm, out_sem.at[3]))
    outs[-1].start()

    total = part[rep] + core_got[place]
    for r in range(1, chips):
        x_copy(r).wait()
        total = total + unpacked(x_got[r - 1].astype(F32))
    wg_ref[...] = total[:, :piece] * (rows_here * n * replicas) ** (-0.5)
    outs.append(pltpu.make_async_copy(wg_ref, wg_hbm, out_sem.at[4]))
    outs[-1].start()

    def sent(t, carry):
        for h in range(CUTS):

            @pl.when((a - t >= 0) & (a + 1 < line))
            def _():
                up_copy(t, mall.at[me], h).wait_send()

            @pl.when((a + t < line) & (a > 0))
            def _():
                down_copy(t, mall.at[me], h).wait_send()

            side_copy(t, mall.at[me], h).wait_send()
        return carry

    lax.fori_loop(0, line, sent, 0)
    mirror_copy().wait_send()

    def weight_sent(t, carry):
        @pl.when((row - t >= 0) & (row + 1 < near_line))
        def _():
            fup_copy(t).wait_send()

        @pl.when((row + t < near_line) & (row > 0))
        def _():
            fdown_copy(t).wait_send()

        fside_copy(t).wait_send()
        return carry

    lax.fori_loop(0, near_line, weight_sent, 0)
    if shared:

        def passed(src, carry):
            fx_copy(src).wait_send()
            fcore_copy(src, 0).wait_send()
            fcore_copy(src, 1).wait_send()
            return carry

        lax.fori_loop(0, near, passed, 0)
    for copy in outs:
        copy.wait()


def finish_kernel(*refs):
    ins, outs, held = refs[:5], refs[5:10], refs[10:15]
    in_sem, out_sem = refs[15:]
    first = [pltpu.make_async_copy(ins[i], held[i], in_sem.at[i]) for i in range(5)]
    second = [pltpu.make_async_copy(held[i], outs[i], out_sem.at[i]) for i in range(5)]
    for copy in first:
        copy.start()
    for i in range(5):
        first[i].wait()
        second[i].start()
    for copy in second:
        copy.wait()


def fused(merged_grad, merged_owner, merger_pre, fc2_weight, query, key_states, value_states, out_grad, position):
    rows_here, width = merged_grad.shape
    n, replicas = lax.axis_size("ctx"), lax.axis_size("dp")
    slots, units = merger_pre.shape
    mine = units // n
    line = n // SIDES
    near = n // 2
    near_line = line // 2
    block = SIDES * rows_here
    piece = width // replicas
    chips = replicas // 2
    span_out = -(-piece // LANES) * LANES
    tight = piece % LANES * 2 == LANES and mine % 32 == 0
    across = (mine // 2, 2 * piece) if tight else (mine, span_out)
    parts = replicas if chips == 2 and mine % (16 * replicas) == 0 else 1
    vmem = pl.BlockSpec(memory_space=pltpu.VMEM)
    hbm = pl.BlockSpec(memory_space=pl.ANY)
    dma = pltpu.SemaphoreType.DMA
    like = jax.ShapeDtypeStruct(query.shape, BF16)
    shapes = [
        jax.ShapeDtypeStruct((slots, units), BF16),
        jax.ShapeDtypeStruct((mine, piece), F32),
        like,
        like,
        like,
    ]
    results = pl.pallas_call(
        functools.partial(fused_kernel, n, replicas),
        in_specs=[hbm, vmem] + [hbm] * 6 + [vmem],
        out_specs=[hbm] * 5,
        out_shape=shapes,
        scratch_shapes=[
            pltpu.VMEM((n, rows_here, width), BF16),
            pltpu.VMEM((n, 1, rows_here), jnp.int32),
            pltpu.VMEM((slots, units), BF16),
            pltpu.VMEM((slots, units // 2), F32),
            pltpu.VMEM((units, slots), BF16),
            pltpu.VMEM((mine, n * slots), BF16),
            pltpu.VMEM((near, parts, mine // parts, width), BF16),
            pltpu.VMEM((parts, mine // parts, width), BF16),
            pltpu.VMEM((line, 8, block), F32),
            pltpu.VMEM((slots, width), BF16),
            pltpu.VMEM((mine, line * block), BF16),
            pltpu.VMEM((line, mine, block), F32),
            pltpu.VMEM((mine, block), BF16),
            pltpu.VMEM((near, mine, slots), BF16),
            pltpu.VMEM((near, mine, slots), BF16),
            pltpu.VMEM((slots, units), BF16),
            pltpu.VMEM((mine, width), F32),
            pltpu.VMEM((replicas, mine, span_out), F32),
            pltpu.VMEM((chips, mine, span_out), F32),
            pltpu.VMEM((max(chips - 1, 1), *across), F32),
            pltpu.VMEM((max(chips - 1, 1), *across), F32),
            pltpu.VMEM((mine, piece), F32),
        ]
        + [pltpu.VMEM(query.shape, BF16)] * 7
        + [
            pltpu.VMEM((query.shape[0], LANES), F32),
            pltpu.VMEM((query.shape[0], LANES), F32),
            dma((n, CUTS)),
            dma((line, CUTS)),
            dma((line, CUTS)),
            dma((line, CUTS)),
            dma((n - 1,)),
            dma((n - 1,)),
            dma((n - 1,)),
            dma((n - 1,)),
            dma((near, parts)),
            dma((1,)),
            dma((near_line,)),
            dma((near_line,)),
            dma((near_line,)),
            dma((near,)),
            dma((near, 2)),
            dma((near - 1,)),
            dma((near - 1,)),
            dma((chips,)),
            dma((chips,)),
            dma((max(chips - 1, 1),)),
            dma((max(chips - 1, 1),)),
            dma((10,)),
            dma((5,)),
        ],
        compiler_params=pltpu.CompilerParams(
            collective_id=0, has_side_effects=True, vmem_limit_bytes=60 * 2**20
        ),
        name="fused",
    )(
        merged_grad,
        merged_owner.reshape(1, rows_here),
        merger_pre,
        fc2_weight.reshape(parts, mine // parts, width),
        query,
        key_states,
        value_states,
        out_grad,
        position,
    )
    return tuple(
        pl.pallas_call(
            finish_kernel,
            in_specs=[hbm] * 5,
            out_specs=[hbm] * 5,
            out_shape=shapes,
            scratch_shapes=[pltpu.VMEM(shape.shape, shape.dtype) for shape in shapes] + [dma((5,)), dma((5,))],
            name="finish",
        )(*results)
    )


def solution(mesh):
    every = P(("dp", "ctx"), None)
    return jax.shard_map(
        fused,
        mesh=mesh,
        in_specs=(every, every, every, P("ctx", None)) + (every,) * 4 + (P(None, ("dp", "ctx")),),
        out_specs=(every, P("ctx", "dp")) + (every,) * 3,
        check_vma=False,
    )
```

```python
import functools
import math

import jax
import jax.numpy as jnp
from jax import lax
from jax.experimental import pallas as pl
from jax.experimental.pallas import tpu as pltpu
from jax.sharding import PartitionSpec as P

HEAD = 80
WIN = 64
LANES = 128
SIDES = 2
CUTS = 2
F32 = jnp.float32
BF16 = jnp.bfloat16
MESH = pl.DeviceIdType.MESH
NT = (((1,), (1,)), ((), ()))
TN = (((0,), (0,)), ((), ()))
NN = (((1,), (0,)), ((), ()))


def dot(a, b, dims=NN):
    return lax.dot_general(a, b, dims, preferred_element_type=F32)


def spread(table, width):
    shape = (LANES, width)
    lane = lax.broadcasted_iota(jnp.int32, shape, 1) % HEAD
    pick = (lane == lax.broadcasted_iota(jnp.int32, shape, 0)).astype(F32).astype(BF16)
    high = table.astype(BF16)
    rest = table - high.astype(F32)
    mid = rest.astype(BF16)
    low = (rest - mid.astype(F32)).astype(BF16)
    return dot(high, pick) + dot(mid, pick) + dot(low, pick)


def rope_tables(pos_ref, c_ref, s_ref):
    count = pos_ref.shape[1]
    half, quarter = HEAD // 2, HEAD // 4
    unit = lax.broadcasted_iota(jnp.int32, (LANES, count), 0)
    rows = pos_ref[0:1, :].astype(F32)
    cols = pos_ref[1:2, :].astype(F32)
    rank = (unit % half % quarter).astype(F32)
    freq = jnp.exp(rank * (-4.0 / HEAD * math.log(10000.0)))
    angles = jnp.where(unit % half < quarter, rows, cols) * freq
    c_ref[...] = jnp.transpose(jnp.cos(angles))
    s_ref[...] = jnp.transpose(jnp.where(unit < half, -1.0, 1.0) * jnp.sin(angles))


def attention_part(at, over, refs, c_ref, s_ref, outs):
    q_ref, k_ref, v_ref, g_ref = refs
    dq_ref, dk_ref, dv_ref = outs
    width = over.size
    heads = width // HEAD
    half = HEAD // 2
    cosine = spread(c_ref[at, :], width)
    sine = spread(s_ref[at, :], width)
    lane = lax.broadcasted_iota(jnp.int32, (WIN, width), 1)
    first = lane % HEAD < half

    def swap(x):
        return jnp.where(first, pltpu.roll(x, width - half, 1), pltpu.roll(x, half, 1))

    def rotated(x):
        return (x * cosine + swap(x) * sine).astype(BF16)

    def unrotated(x):
        return (x * cosine - swap(x) * sine).astype(BF16)

    q = rotated(q_ref[at, over].astype(F32))
    k = rotated(k_ref[at, over].astype(F32))
    v = v_ref[at, over]
    g = g_ref[at, over]
    factor = HEAD ** (-0.5)
    dq, dk, dv = {}, {}, {}

    def add(into, tile, value):
        for i in range(value.shape[1] // LANES):
            part = value[:, i * LANES : (i + 1) * LANES]
            into[tile + i] = into[tile + i] + part if tile + i in into else part

    for head in range(heads):
        tile = head * HEAD // LANES
        end = -(-(head + 1) * HEAD // LANES)
        lo, hi = tile * LANES, end * LANES
        here = lax.broadcasted_iota(jnp.int32, (1, hi - lo), 1) + lo
        mask = ((here >= head * HEAD) & (here < (head + 1) * HEAD)).astype(F32).astype(BF16)
        qm = q[:, lo:hi] * mask
        km = k[:, lo:hi] * mask
        gm = g[:, lo:hi] * mask
        scores = dot(qm, k[:, lo:hi], NT) * factor
        weight = jnp.exp(scores - jnp.max(scores, axis=1, keepdims=True))
        probs = weight * (1.0 / jnp.sum(weight, axis=1, keepdims=True))
        probs_b = probs.astype(BF16)
        prob_grad = dot(gm, v[:, lo:hi], NT)
        delta = jnp.sum(probs_b.astype(F32) * prob_grad, axis=1, keepdims=True)
        score_grad = (probs * (prob_grad - delta)).astype(BF16)
        add(dv, tile, dot(probs_b, gm, TN))
        add(dq, tile, dot(score_grad, km, NN))
        add(dk, tile, dot(score_grad, qm, TN))

    def joined(parts):
        return jnp.concatenate([parts[i] for i in range(width // LANES)], axis=1)

    dq_ref[at, over] = unrotated(joined(dq) * factor)
    dk_ref[at, over] = unrotated(joined(dk) * factor)
    dv_ref[at, over] = joined(dv).astype(BF16)


def fused_kernel(
    n,
    replicas,
    m_hbm,
    o_ref,
    p_hbm,
    w_hbm,
    q_hbm,
    k_hbm,
    v_hbm,
    g_hbm,
    pos_ref,
    h_ref,
    wg_ref,
    dq_ref,
    dk_ref,
    dv_ref,
    mall,
    owners,
    pre,
    slope,
    pre_send,
    pre_got,
    fall,
    w_ref,
    code,
    ranks,
    slotted,
    hid,
    linear_ref,
    act_ref,
    hid_out,
    hid_got,
    full,
    part,
    core_got,
    x_out,
    x_got,
    q_ref,
    k_ref,
    v_ref,
    g_ref,
    c_ref,
    s_ref,
    m_recv,
    up_sem,
    down_sem,
    side_sem,
    o_send,
    o_recv,
    p_send,
    p_recv,
    f_recv,
    mirror_sem,
    fup_sem,
    fdown_sem,
    fside_sem,
    fx_sem,
    fcore_sem,
    h_send,
    h_recv,
    c_send,
    c_recv,
    x_send,
    x_recv,
    local_sem,
):
    line = n // SIDES
    near = n // 2
    near_line = line // 2
    rows_here, width = m_hbm.shape
    slots, units = pre.shape
    mine = units // n
    parts = w_hbm.shape[0]
    shared = parts > 1
    block = SIDES * rows_here
    patches, features = q_ref.shape
    chips = replicas // 2
    me = lax.axis_index("ctx")
    rep = lax.axis_index("dp")
    a, b = me // SIDES, me % SIDES
    side, row = a // near_line, a % near_line
    here = me % near
    mirror = (me + near) % n
    partner = rep // 2 * 2 + 1 - rep % 2
    core, place = rep % 2, rep // 2
    q_own = rep if shared else 0
    q_far = (rep + 2) % replicas if shared else 0

    barrier = pltpu.get_barrier_semaphore()
    for r in range(1, n):
        pl.semaphore_signal(barrier, inc=1, device_id={"dp": rep, "ctx": (me + r) % n}, device_id_type=MESH)
    pl.semaphore_signal(barrier, inc=1, device_id={"dp": partner, "ctx": me}, device_id_type=MESH)
    for r in range(1, chips):
        pl.semaphore_signal(
            barrier, inc=1, device_id={"dp": (rep + 2 * r) % replicas, "ctx": me}, device_id_type=MESH
        )
    locals_ = [
        pltpu.make_async_copy(p_hbm, pre, local_sem.at[0]),
        pltpu.make_async_copy(q_hbm, q_ref, local_sem.at[1]),
        pltpu.make_async_copy(k_hbm, k_ref, local_sem.at[2]),
        pltpu.make_async_copy(v_hbm, v_ref, local_sem.at[3]),
        pltpu.make_async_copy(g_hbm, g_ref, local_sem.at[4]),
        pltpu.make_async_copy(m_hbm, mall.at[me], local_sem.at[5]),
        pltpu.make_async_copy(w_hbm, w_ref, local_sem.at[6]),
        pltpu.make_async_copy(o_ref, owners.at[me], local_sem.at[7]),
    ]
    for copy in locals_:
        copy.start()
    pl.semaphore_wait(barrier, n - 1 + chips)

    def send(src, dst, send_sem, recv_sem, ctx=None, dp=None):
        where = {"dp": rep if dp is None else dp, "ctx": me if ctx is None else ctx}
        return pltpu.make_async_remote_copy(
            src_ref=src,
            dst_ref=dst,
            send_sem=send_sem,
            recv_sem=recv_sem,
            device_id=where,
            device_id_type=MESH,
        )

    def owner_copy(r):
        return send(o_ref, owners.at[me], o_send.at[r - 1], o_recv.at[r - 1], ctx=(me + r) % n)

    def unit_rows(peer):
        return pre_send.at[pl.ds(pl.multiple_of(peer * mine, 16), mine), :]

    def pre_place():
        return pre_got.at[:, pl.ds(pl.multiple_of(me * slots, LANES), slots)]

    def pre_copy(r):
        peer = (me + r) % n
        return send(unit_rows(peer), pre_place(), p_send.at[r - 1], p_recv.at[r - 1], ctx=peer)

    def turn_side(phase):
        return side if phase == 0 else 1 - side

    def half_lanes(phase):
        return pl.ds(pl.multiple_of(turn_side(phase) * (slots // 2), LANES), slots // 2)

    def hidden_copy(r, phase):
        to = (here + r) % near
        lanes = half_lanes(phase)
        return send(
            hid_out.at[to, :, lanes],
            hid_got.at[here, :, lanes],
            h_send.at[r - 1, phase],
            h_recv.at[r - 1, phase],
            ctx=side * near + to,
        )

    def cut(h):
        return pl.ds(h * (rows_here // CUTS), rows_here // CUTS)

    def up_copy(t, ref, h):
        at = (a - t) * SIDES + b
        return send(ref.at[cut(h)], mall.at[at, cut(h)], up_sem.at[t, h], m_recv.at[at, h], ctx=me + SIDES)

    def down_copy(t, ref, h):
        at = (a + t) * SIDES + b
        return send(ref.at[cut(h)], mall.at[at, cut(h)], down_sem.at[t, h], m_recv.at[at, h], ctx=me - SIDES)

    def side_copy(at, ref, h):
        src = at * SIDES + b
        to = a * SIDES + 1 - b
        return send(ref.at[cut(h)], mall.at[src, cut(h)], side_sem.at[at, h], m_recv.at[src, h], ctx=to)

    def m_arrived(src, h):
        ref = mall.at[src, cut(h)]
        send(ref, ref, up_sem.at[0, 0], m_recv.at[src, h], ctx=a * SIDES + 1 - b).wait_recv()

    def mirror_copy():
        return send(
            w_hbm.at[q_own], fall.at[here, q_own], mirror_sem.at[0], f_recv.at[here, q_own], ctx=mirror
        )

    def fup_copy(t):
        at = (row - t) * SIDES + b
        ref = fall.at[at, q_own]
        return send(ref, ref, fup_sem.at[t], f_recv.at[at, q_own], ctx=me + SIDES)

    def fdown_copy(t):
        at = (row + t) * SIDES + b
        ref = fall.at[at, q_own]
        return send(ref, ref, fdown_sem.at[t], f_recv.at[at, q_own], ctx=me - SIDES)

    def fside_copy(at):
        src = at * SIDES + b
        ref = fall.at[src, q_own]
        return send(ref, ref, fside_sem.at[at], f_recv.at[src, q_own], ctx=a * SIDES + 1 - b)

    def fx_copy(src):
        ref = fall.at[src, q_own]
        return send(ref, ref, fx_sem.at[src], f_recv.at[src, q_own], dp=q_far)

    def fcore_copy(src, which):
        at = (q_own, q_far)[which]
        ref = fall.at[src, at]
        return send(ref, ref, fcore_sem.at[src, which], f_recv.at[src, at], dp=partner)

    def f_arrived(src, at):
        ref = fall.at[src, at]
        send(ref, ref, fup_sem.at[0], f_recv.at[src, at], ctx=a * SIDES + 1 - b).wait_recv()

    def core_copy(x):
        return send(
            part.at[2 * x + 1 - core], core_got.at[x], c_send.at[x], c_recv.at[x], dp=partner
        )

    def x_copy(r):
        peer = (rep + 2 * r) % replicas
        return send(x_out.at[r - 1], x_got.at[r - 1], x_send.at[r - 1], x_recv.at[r - 1], dp=peer)

    def when(condition, body):
        pl.when(condition)(body)

    for r in range(1, n):
        owner_copy(r).start()
    for h in range(CUTS):
        when(a + 1 < line, lambda h=h: up_copy(0, m_hbm, h).start())
        when(a > 0, lambda h=h: down_copy(0, m_hbm, h).start())
        side_copy(a, m_hbm, h).start()
    mirror_copy().start()

    locals_[0].wait()

    def turn(j, carry):
        over = pl.ds(pl.multiple_of(j * LANES, LANES), LANES)
        pre_send[over, :] = jnp.transpose(pre[:, over].astype(F32)).astype(BF16)
        return carry

    lax.fori_loop(0, units // LANES, turn, 0)
    own_pre = pltpu.make_async_copy(unit_rows(me), pre_place(), local_sem.at[8])
    own_pre.start()
    rope_tables(pos_ref, c_ref, s_ref)
    full[...] = jnp.zeros_like(full)
    slotted[...] = jnp.zeros_like(slotted)
    for copy in locals_[1:5]:
        copy.wait()

    def both(t, at, count, body):
        if t == 0:
            body(at, None)
        else:
            when(at - t >= 0, lambda: body(at - t, True))
            when(at + t < count, lambda: body(at + t, False))

    def send_pre():
        for r in range(1, n):
            pre_copy(r).start()

    def token_event(t):
        def body(at, below):
            src = at * SIDES + b
            ref = mall.at[src]
            for h in range(CUTS):
                m_arrived(src, h)
                if below:
                    when(a + 1 < line, lambda h=h: up_copy(t, ref, h).start())
                else:
                    when(a > 0, lambda h=h: down_copy(t, ref, h).start())
                side_copy(at, ref, h).start()

        both(t, a, line, body)

    def across(src):
        if shared:
            fx_copy(src).start()
            fcore_copy(src, 0).start()

    def weight_event(t):
        def body(at, below):
            src = at * SIDES + b
            f_arrived(src, q_own)
            if below is not False:
                when(row + 1 < near_line, lambda: fup_copy(t).start())
            if below is not True:
                when(row > 0, lambda: fdown_copy(t).start())
            across(src)

        both(t, row, near_line, body)

    def weight_turn(t):
        both(t, row, near_line, lambda at, below: fside_copy(at).start())

    def weight_side_event(t):
        def body(at, below):
            src = at * SIDES + 1 - b
            f_arrived(src, q_own)
            across(src)

        both(t, row, near_line, body)

    def weight_far_event(t, other):
        def body(at, below):
            src = at * SIDES + (1 - b if other else b)
            if shared:
                f_arrived(src, q_far)
                fcore_copy(src, 1).start()

        both(t, row, near_line, body)

    def event(kind, *given):
        return functools.partial(kind, *given)

    order = [
        (1, event(token_event, 1)),
        (2, event(weight_event, 0)),
        (2, event(weight_turn, 0)),
        (4, event(token_event, 2)),
        (4, send_pre),
        (5, event(weight_side_event, 0)),
        (6, event(weight_event, 1)),
        (6, event(weight_turn, 1)),
        (6, event(weight_far_event, 0, False)),
    ]

    halves = 2
    span = features // halves
    steps = patches // WIN * halves

    def attend(i, carry):
        at = pl.ds(pl.multiple_of(i // halves * WIN, WIN), WIN)
        over = pl.ds(pl.multiple_of(i % halves * span, LANES), span)
        attention_part(
            at, over, (q_ref, k_ref, v_ref, g_ref), c_ref, s_ref, (dq_ref, dk_ref, dv_ref)
        )
        for step in range(steps):
            todo = [run for index, run in order if index == step]
            if todo:
                when(i == step, lambda todo=todo: [run() for run in todo] and None)
        return carry

    lax.fori_loop(0, steps, attend, 0)
    far = (1 - side) * (units // 2)

    def incline(j, carry):
        x = pre[:, pl.ds(pl.multiple_of(far + j * LANES, LANES), LANES)].astype(F32)
        cdf = 0.5 * (1.0 + lax.erf(x * 0.5**0.5))
        slope[:, pl.ds(pl.multiple_of(j * LANES, LANES), LANES)] = cdf + x * jnp.exp(-0.5 * x * x) * (
            2.0 * math.pi
        ) ** (-0.5)
        return carry

    lax.fori_loop(0, units // 2 // LANES, incline, 0)

    for copy in locals_[5:]:
        copy.wait()
    for r in range(1, n):
        owner_copy(r).wait()
    padded = -(-n // 16) * 16
    earlier = lax.broadcasted_iota(jnp.int32, (rows_here, rows_here), 0) < lax.broadcasted_iota(
        jnp.int32, (rows_here, rows_here), 1
    )
    earlier = earlier.astype(F32).astype(BF16)
    names = lax.broadcasted_iota(jnp.int32, (padded, rows_here), 0)
    base = jnp.zeros((padded, 1), F32)
    cap = slots // n
    mine_only = lax.broadcasted_iota(jnp.int32, (padded, 1), 0) == me
    lane_of = lax.broadcasted_iota(jnp.int32, (1, slots), 1)
    in_source = (lane_of % cap).astype(F32)
    slot_of = jnp.full((1, slots), -1.0, F32)
    for s in range(n):
        onehot = (names == owners[s]).astype(F32)
        count = dot(onehot.astype(BF16), earlier)
        named = names.astype(F32)
        position = jnp.sum(onehot * (count + base + named * float(slots)), axis=0, keepdims=True)
        ranked = jnp.sum(onehot * (count + named * float(slots // 2)), axis=0, keepdims=True)
        tally = jnp.sum(onehot, axis=1, keepdims=True)
        start = jnp.sum(jnp.where(mine_only, base, 0.0), axis=0, keepdims=True)
        held = jnp.sum(jnp.where(mine_only, tally, 0.0), axis=0, keepdims=True)
        spot_of = jnp.where(in_source < held, start + in_source, -1.0)
        slot_of = jnp.where(lane_of // cap == s, spot_of, slot_of)
        base = base + tally
        lo = s % SIDES * rows_here
        code[s // SIDES, :, lo : lo + rows_here] = jnp.broadcast_to(position, (8, rows_here))
        ranks[s // SIDES, :, lo : lo + rows_here] = jnp.broadcast_to(
            ranked + float(s % near * cap), (8, rows_here)
        )
    standing = lax.broadcasted_iota(jnp.int32, (slots, block), 0).astype(F32)

    def landing(o, t):
        first = (o * slots).astype(F32)
        return (standing == code[t, 0:1, :] - first).astype(F32).astype(BF16)

    def nth(d):
        low = jnp.where(d <= a, a - d, d)
        flip = line - 1 - a
        high = line - 1 - jnp.where(d <= flip, flip - d, d)
        return jnp.where(side == 0, low, high)

    def gathered(t):
        return jnp.concatenate([mall[t * SIDES + i] for i in range(SIDES)], axis=0)

    def slotting(t, rows):
        slotted[...] += dot(landing(me, t), rows).astype(BF16)

    def early(d, carry):
        t = nth(d)
        for h in range(CUTS):
            m_arrived(t * SIDES + 1 - b, h)
        rows = gathered(t)
        linear_ref[t] = dot(w_ref[...].reshape(mine, width), rows, NT)
        slotting(t, rows)
        return carry

    def activation(t):
        spots = jnp.concatenate([landing(jnp.int32(o), t) for o in range(n)], axis=0)
        x = dot(pre_got[...], spots)
        cdf = 0.5 * (1.0 + lax.erf(x * 0.5**0.5))
        incline = cdf + x * jnp.exp(-0.5 * x * x) * (2.0 * math.pi) ** (-0.5)
        return (x * cdf).astype(BF16), incline

    ranking = lax.broadcasted_iota(jnp.int32, (slots // 2, block), 0).astype(F32)

    def send_hidden(phase):
        first = turn_side(phase) * near_line
        lanes = half_lanes(phase)
        blocks = pl.ds(pl.multiple_of(first * block, LANES), near_line * block)

        def outgoing(i, carry):
            shift = ((side * near + i) * (slots // 2)).astype(F32)
            spots = [ranking == ranks[first + j, 0:1, :] - shift for j in range(near_line)]
            spots = jnp.concatenate([spot.astype(F32).astype(BF16) for spot in spots], axis=1)
            hid_out[i, :, lanes] = dot(hid[:, blocks], spots, NT).astype(BF16)
            return carry

        lax.fori_loop(0, near, outgoing, 0)
        for r in range(1, near):
            hidden_copy(r, phase).start()
        own_hidden(phase).start()

    def own_hidden(phase):
        lanes = half_lanes(phase)
        return pltpu.make_async_copy(
            hid_out.at[here, :, lanes], hid_got.at[here, :, lanes], local_sem.at[9 + phase]
        )

    def hid_place(t):
        return pl.ds(pl.multiple_of(t * block, LANES), block)

    def late(d, carry):
        t = nth(d)
        act, incline = activation(t)
        hid[:, hid_place(t)] = (linear_ref[t] * incline).astype(BF16)
        full[...] += dot(act, gathered(t))
        return carry

    lax.fori_loop(0, line - 1, early, 0)
    for t in range(2, near_line):
        weight_event(t)
        weight_turn(t)
    weight_far_event(0, True)
    for t in range(1, near_line):
        weight_far_event(t, False)
    for t in range(3, line):
        token_event(t)
    for t in range(1, near_line):
        weight_side_event(t)
    for r in range(1, n):
        pre_copy(r).wait()
    own_pre.wait()
    lax.fori_loop(0, near_line, late, 0)
    send_hidden(0)
    lax.fori_loop(near_line, line - 1, late, 0)
    last = nth(jnp.int32(line - 1))
    act_ref[...], linear_ref[last] = activation(last)
    for h in range(CUTS):
        m_arrived(last * SIDES + 1 - b, h)
    full[...] += dot(act_ref[...], gathered(last))


    piece = width // replicas
    span_out = part.shape[2]
    for d in range(replicas):
        lo = d * piece // LANES * LANES
        hi = -(-(d + 1) * piece // LANES) * LANES
        shift = d * piece - lo
        value = full[:, lo:hi]
        if shift:
            value = pltpu.roll(value, hi - lo - shift, 1)
        part[d] = value[:, :span_out]
    for x in range(chips):
        core_copy(x).start()
    late_rows = gathered(last)
    late_linear = dot(w_ref[...].reshape(mine, width), late_rows, NT)
    hid[:, hid_place(last)] = (late_linear * linear_ref[last]).astype(BF16)

    tight = x_out.shape[1] < mine
    rest = piece % LANES
    whole = piece - rest
    lane = lax.broadcasted_iota(jnp.int32, (mine // 2, LANES), 1)

    def packed(value):
        if not tight:
            return value
        top, low = value[: mine // 2], value[mine // 2 :]
        low = pltpu.roll(low, rest, 1)
        seam = jnp.where(lane < rest, top[:, whole:], low[:, :LANES])
        return jnp.concatenate([top[:, :whole], seam, low[:, LANES:]], axis=1)

    def unpacked(value):
        if not tight:
            return value
        low = pltpu.roll(value[:, whole:], span_out - rest, 1)
        return jnp.concatenate([value[:, :span_out], low], axis=0)

    for x in range(chips):
        core_copy(x).wait()
    for r in range(1, chips):
        x = (place + r) % chips
        x_out[r - 1] = packed(part[2 * x + core] + core_got[x]).astype(x_out.dtype)
        x_copy(r).start()

    send_hidden(1)


    groups = next(g for g in range(near_line, 0, -1) if near_line % g == 0 and units // 2 // g % LANES == 0)
    run, each = near // groups, units // 2 // groups

    def linear(g, carry):
        if shared:

            def await_rest(i, carry):
                for other in (partner, (partner + 2) % replicas):
                    f_arrived(g * run + i, other)
                return carry

            lax.fori_loop(0, run, await_rest, 0)
        weight = fall[pl.ds(g * run, run)].reshape(each, width)
        over = pl.ds(pl.multiple_of(g * each, LANES), each)
        to = pl.ds(pl.multiple_of(far + g * each, LANES), each)
        h_ref[:, to] = (dot(slotted[...], weight, NT) * slope[:, over]).astype(BF16)
        return carry

    slotting(last, gathered(last))
    for t in range(1, near_line):
        weight_far_event(t, True)
    lax.fori_loop(0, groups, linear, 0)

    for phase in range(2):
        own_hidden(phase).wait()
        for r in range(1, near):
            hidden_copy(r, phase).wait()
    spot = lax.broadcasted_iota(jnp.int32, (slots, slots), 0).astype(F32) == slot_of
    spot = spot.astype(F32).astype(BF16)

    def settle(g, carry):
        rows = hid_got[pl.ds(g * run, run)].reshape(each, slots)
        to = pl.ds(pl.multiple_of(side * (units // 2) + g * each, LANES), each)
        h_ref[:, to] = dot(spot, rows, NT).astype(BF16)
        return carry

    lax.fori_loop(0, groups, settle, 0)

    total = part[rep] + core_got[place]
    for r in range(1, chips):
        x_copy(r).wait()
        total = total + unpacked(x_got[r - 1].astype(F32))
    wg_ref[...] = total[:, :piece] * (rows_here * n * replicas) ** (-0.5)

    def sent(t, carry):
        for h in range(CUTS):

            @pl.when((a - t >= 0) & (a + 1 < line))
            def _():
                up_copy(t, mall.at[me], h).wait_send()

            @pl.when((a + t < line) & (a > 0))
            def _():
                down_copy(t, mall.at[me], h).wait_send()

            side_copy(t, mall.at[me], h).wait_send()
        return carry

    lax.fori_loop(0, line, sent, 0)
    mirror_copy().wait_send()

    def weight_sent(t, carry):
        @pl.when((row - t >= 0) & (row + 1 < near_line))
        def _():
            fup_copy(t).wait_send()

        @pl.when((row + t < near_line) & (row > 0))
        def _():
            fdown_copy(t).wait_send()

        fside_copy(t).wait_send()
        return carry

    lax.fori_loop(0, near_line, weight_sent, 0)
    if shared:

        def passed(src, carry):
            fx_copy(src).wait_send()
            fcore_copy(src, 0).wait_send()
            fcore_copy(src, 1).wait_send()
            return carry

        lax.fori_loop(0, near, passed, 0)


def finish_kernel(*refs):
    count = len(refs) // 2
    copies = [pltpu.make_async_copy(refs[i], refs[count + i], refs[-1].at[i]) for i in range(count)]
    for copy in copies:
        copy.start()
    for copy in copies:
        copy.wait()


def fused(merged_grad, merged_owner, merger_pre, fc2_weight, query, key_states, value_states, out_grad, position):
    rows_here, width = merged_grad.shape
    n, replicas = lax.axis_size("ctx"), lax.axis_size("dp")
    slots, units = merger_pre.shape
    mine = units // n
    line = n // SIDES
    near = n // 2
    near_line = line // 2
    block = SIDES * rows_here
    piece = width // replicas
    chips = replicas // 2
    span_out = -(-piece // LANES) * LANES
    tight = piece % LANES * 2 == LANES and mine % 32 == 0
    across = (mine // 2, 2 * piece) if tight else (mine, span_out)
    parts = replicas if chips == 2 and mine % (16 * replicas) == 0 else 1
    vmem = pl.BlockSpec(memory_space=pltpu.VMEM)
    hbm = pl.BlockSpec(memory_space=pl.ANY)
    dma = pltpu.SemaphoreType.DMA
    like = jax.ShapeDtypeStruct(query.shape, BF16)
    shapes = [
        jax.ShapeDtypeStruct((slots, units), BF16),
        jax.ShapeDtypeStruct((mine, piece), F32),
        like,
        like,
        like,
    ]
    results = pl.pallas_call(
        functools.partial(fused_kernel, n, replicas),
        in_specs=[hbm, vmem] + [hbm] * 6 + [vmem],
        out_specs=[vmem] * 5,
        out_shape=[pltpu.VMEM(shape.shape, shape.dtype) for shape in shapes],
        scratch_shapes=[
            pltpu.VMEM((n, rows_here, width), BF16),
            pltpu.VMEM((n, 1, rows_here), jnp.int32),
            pltpu.VMEM((slots, units), BF16),
            pltpu.VMEM((slots, units // 2), F32),
            pltpu.VMEM((units, slots), BF16),
            pltpu.VMEM((mine, n * slots), BF16),
            pltpu.VMEM((near, parts, mine // parts, width), BF16),
            pltpu.VMEM((parts, mine // parts, width), BF16),
            pltpu.VMEM((line, 8, block), F32),
            pltpu.VMEM((line, 8, block), F32),
            pltpu.VMEM((slots, width), BF16),
            pltpu.VMEM((mine, line * block), BF16),
            pltpu.VMEM((line, mine, block), F32),
            pltpu.VMEM((mine, block), BF16),
            pltpu.VMEM((near, mine, slots), BF16),
            pltpu.VMEM((near, mine, slots), BF16),
            pltpu.VMEM((mine, width), F32),
            pltpu.VMEM((replicas, mine, span_out), F32),
            pltpu.VMEM((chips, mine, span_out), F32),
            pltpu.VMEM((max(chips - 1, 1), *across), BF16),
            pltpu.VMEM((max(chips - 1, 1), *across), BF16),
        ]
        + [pltpu.VMEM(query.shape, BF16)] * 4
        + [
            pltpu.VMEM((query.shape[0], LANES), F32),
            pltpu.VMEM((query.shape[0], LANES), F32),
            dma((n, CUTS)),
            dma((line, CUTS)),
            dma((line, CUTS)),
            dma((line, CUTS)),
            dma((n - 1,)),
            dma((n - 1,)),
            dma((n - 1,)),
            dma((n - 1,)),
            dma((near, parts)),
            dma((1,)),
            dma((near_line,)),
            dma((near_line,)),
            dma((near_line,)),
            dma((near,)),
            dma((near, 2)),
            dma((near - 1, 2)),
            dma((near - 1, 2)),
            dma((chips,)),
            dma((chips,)),
            dma((max(chips - 1, 1),)),
            dma((max(chips - 1, 1),)),
            dma((11,)),
        ],
        compiler_params=pltpu.CompilerParams(
            collective_id=0, has_side_effects=True, vmem_limit_bytes=60 * 2**20
        ),
        name="fused",
    )(
        merged_grad,
        merged_owner.reshape(1, rows_here),
        merger_pre,
        fc2_weight.reshape(parts, mine // parts, width),
        query,
        key_states,
        value_states,
        out_grad,
        position,
    )
    return tuple(
        pl.pallas_call(
            finish_kernel,
            in_specs=[vmem] * 5,
            out_specs=[hbm] * 5,
            out_shape=shapes,
            scratch_shapes=[dma((5,))],
            compiler_params=pltpu.CompilerParams(vmem_limit_bytes=2**20),
            name="finish",
        )(*results)
    )


def solution(mesh):
    every = P(("dp", "ctx"), None)
    return jax.shard_map(
        fused,
        mesh=mesh,
        in_specs=(every, every, every, P("ctx", None)) + (every,) * 4 + (P(None, ("dp", "ctx")),),
        out_specs=(every, P("ctx", "dp")) + (every,) * 3,
        check_vma=False,
    )
```

```python
import functools
import math

import jax
import jax.numpy as jnp
from jax import lax
from jax.experimental import pallas as pl
from jax.experimental.pallas import tpu as pltpu
from jax.sharding import PartitionSpec as P

HEAD = 80
WIN = 64
LANES = 128
SIDES = 2
CUTS = 2
F32 = jnp.float32
BF16 = jnp.bfloat16
MESH = pl.DeviceIdType.MESH
NT = (((1,), (1,)), ((), ()))
TN = (((0,), (0,)), ((), ()))
NN = (((1,), (0,)), ((), ()))


def dot(a, b, dims=NN):
    return lax.dot_general(a, b, dims, preferred_element_type=F32)


def spread(table, width):
    shape = (LANES, width)
    lane = lax.broadcasted_iota(jnp.int32, shape, 1) % HEAD
    pick = (lane == lax.broadcasted_iota(jnp.int32, shape, 0)).astype(F32).astype(BF16)
    high = table.astype(BF16)
    rest = table - high.astype(F32)
    mid = rest.astype(BF16)
    low = (rest - mid.astype(F32)).astype(BF16)
    return dot(high, pick) + dot(mid, pick) + dot(low, pick)


def rope_tables(pos_ref, c_ref, s_ref):
    count = pos_ref.shape[1]
    half, quarter = HEAD // 2, HEAD // 4
    unit = lax.broadcasted_iota(jnp.int32, (LANES, count), 0)
    rows = pos_ref[0:1, :].astype(F32)
    cols = pos_ref[1:2, :].astype(F32)
    rank = (unit % half % quarter).astype(F32)
    freq = jnp.exp(rank * (-4.0 / HEAD * math.log(10000.0)))
    angles = jnp.where(unit % half < quarter, rows, cols) * freq
    c_ref[...] = jnp.transpose(jnp.cos(angles))
    s_ref[...] = jnp.transpose(jnp.where(unit < half, -1.0, 1.0) * jnp.sin(angles))


def attention_part(at, over, refs, c_ref, s_ref, outs):
    q_ref, k_ref, v_ref, g_ref = refs
    dq_ref, dk_ref, dv_ref = outs
    width = over.size
    heads = width // HEAD
    half = HEAD // 2
    cosine = spread(c_ref[at, :], width)
    sine = spread(s_ref[at, :], width)
    lane = lax.broadcasted_iota(jnp.int32, (WIN, width), 1)
    first = lane % HEAD < half

    def swap(x):
        return jnp.where(first, pltpu.roll(x, width - half, 1), pltpu.roll(x, half, 1))

    def rotated(x):
        return (x * cosine + swap(x) * sine).astype(BF16)

    def unrotated(x):
        return (x * cosine - swap(x) * sine).astype(BF16)

    q = rotated(q_ref[at, over].astype(F32))
    k = rotated(k_ref[at, over].astype(F32))
    v = v_ref[at, over]
    g = g_ref[at, over]
    factor = HEAD ** (-0.5)
    dq, dk, dv = {}, {}, {}

    def add(into, tile, value):
        for i in range(value.shape[1] // LANES):
            part = value[:, i * LANES : (i + 1) * LANES]
            into[tile + i] = into[tile + i] + part if tile + i in into else part

    for head in range(heads):
        tile = head * HEAD // LANES
        end = -(-(head + 1) * HEAD // LANES)
        lo, hi = tile * LANES, end * LANES
        here = lax.broadcasted_iota(jnp.int32, (1, hi - lo), 1) + lo
        mask = ((here >= head * HEAD) & (here < (head + 1) * HEAD)).astype(F32).astype(BF16)
        qm = q[:, lo:hi] * mask
        km = k[:, lo:hi] * mask
        gm = g[:, lo:hi] * mask
        scores = dot(qm, k[:, lo:hi], NT) * factor
        weight = jnp.exp(scores - jnp.max(scores, axis=1, keepdims=True))
        probs = weight * (1.0 / jnp.sum(weight, axis=1, keepdims=True))
        probs_b = probs.astype(BF16)
        prob_grad = dot(gm, v[:, lo:hi], NT)
        delta = jnp.sum(probs_b.astype(F32) * prob_grad, axis=1, keepdims=True)
        score_grad = (probs * (prob_grad - delta)).astype(BF16)
        add(dv, tile, dot(probs_b, gm, TN))
        add(dq, tile, dot(score_grad, km, NN))
        add(dk, tile, dot(score_grad, qm, TN))

    def joined(parts):
        return jnp.concatenate([parts[i] for i in range(width // LANES)], axis=1)

    dq_ref[at, over] = unrotated(joined(dq) * factor)
    dk_ref[at, over] = unrotated(joined(dk) * factor)
    dv_ref[at, over] = joined(dv).astype(BF16)


def fused_kernel(
    n,
    replicas,
    m_hbm,
    o_ref,
    p_hbm,
    w_hbm,
    q_hbm,
    k_hbm,
    v_hbm,
    g_hbm,
    pos_ref,
    h_ref,
    wg_ref,
    dq_ref,
    dk_ref,
    dv_ref,
    mall,
    owners,
    pre,
    slope,
    pre_send,
    pre_got,
    fall,
    w_ref,
    code,
    ranks,
    slotted,
    hid,
    linear_ref,
    act_ref,
    hid_out,
    hid_got,
    full,
    part,
    core_got,
    x_out,
    x_got,
    q_ref,
    k_ref,
    v_ref,
    g_ref,
    c_ref,
    s_ref,
    m_recv,
    up_sem,
    down_sem,
    side_sem,
    o_send,
    o_recv,
    p_send,
    p_recv,
    f_recv,
    mirror_sem,
    fup_sem,
    fdown_sem,
    fside_sem,
    fx_sem,
    fcore_sem,
    h_send,
    h_recv,
    c_send,
    c_recv,
    x_send,
    x_recv,
    local_sem,
):
    line = n // SIDES
    near = n // 2
    near_line = line // 2
    rows_here, width = m_hbm.shape
    slots, units = pre.shape
    mine = units // n
    parts = w_hbm.shape[0]
    shared = parts > 1
    block = SIDES * rows_here
    patches, features = q_ref.shape
    chips = replicas // 2
    me = lax.axis_index("ctx")
    rep = lax.axis_index("dp")
    a, b = me // SIDES, me % SIDES
    side, row = a // near_line, a % near_line
    here = me % near
    mirror = (me + near) % n
    partner = rep // 2 * 2 + 1 - rep % 2
    core, place = rep % 2, rep // 2
    q_own = rep if shared else 0
    q_far = (rep + 2) % replicas if shared else 0

    barrier = pltpu.get_barrier_semaphore()
    for r in range(1, n):
        pl.semaphore_signal(barrier, inc=1, device_id={"dp": rep, "ctx": (me + r) % n}, device_id_type=MESH)
    pl.semaphore_signal(barrier, inc=1, device_id={"dp": partner, "ctx": me}, device_id_type=MESH)
    for r in range(1, chips):
        pl.semaphore_signal(
            barrier, inc=1, device_id={"dp": (rep + 2 * r) % replicas, "ctx": me}, device_id_type=MESH
        )
    locals_ = [
        pltpu.make_async_copy(p_hbm, pre, local_sem.at[0]),
        pltpu.make_async_copy(q_hbm, q_ref, local_sem.at[1]),
        pltpu.make_async_copy(k_hbm, k_ref, local_sem.at[2]),
        pltpu.make_async_copy(v_hbm, v_ref, local_sem.at[3]),
        pltpu.make_async_copy(g_hbm, g_ref, local_sem.at[4]),
        pltpu.make_async_copy(m_hbm, mall.at[me], local_sem.at[5]),
        pltpu.make_async_copy(w_hbm, w_ref, local_sem.at[6]),
        pltpu.make_async_copy(o_ref, owners.at[me], local_sem.at[7]),
    ]
    for copy in locals_:
        copy.start()
    pl.semaphore_wait(barrier, n - 1 + chips)

    def send(src, dst, send_sem, recv_sem, ctx=None, dp=None):
        where = {"dp": rep if dp is None else dp, "ctx": me if ctx is None else ctx}
        return pltpu.make_async_remote_copy(
            src_ref=src,
            dst_ref=dst,
            send_sem=send_sem,
            recv_sem=recv_sem,
            device_id=where,
            device_id_type=MESH,
        )

    def owner_copy(r):
        return send(o_ref, owners.at[me], o_send.at[r - 1], o_recv.at[r - 1], ctx=(me + r) % n)

    def unit_rows(peer):
        return pre_send.at[pl.ds(pl.multiple_of(peer * mine, 16), mine), :]

    def pre_place():
        return pre_got.at[:, pl.ds(pl.multiple_of(me * slots, LANES), slots)]

    def pre_copy(r):
        peer = (me + r) % n
        return send(unit_rows(peer), pre_place(), p_send.at[r - 1], p_recv.at[r - 1], ctx=peer)

    def turn_side(phase):
        return side if phase == 0 else 1 - side

    def half_lanes(phase):
        return pl.ds(pl.multiple_of(turn_side(phase) * (slots // 2), LANES), slots // 2)

    def hidden_copy(r, phase):
        to = (here + r) % near
        lanes = half_lanes(phase)
        return send(
            hid_out.at[to, :, lanes],
            hid_got.at[here, :, lanes],
            h_send.at[r - 1, phase],
            h_recv.at[r - 1, phase],
            ctx=side * near + to,
        )

    def cut(h):
        return pl.ds(h * (rows_here // CUTS), rows_here // CUTS)

    def up_copy(t, ref, h):
        at = (a - t) * SIDES + b
        return send(ref.at[cut(h)], mall.at[at, cut(h)], up_sem.at[t, h], m_recv.at[at, h], ctx=me + SIDES)

    def down_copy(t, ref, h):
        at = (a + t) * SIDES + b
        return send(ref.at[cut(h)], mall.at[at, cut(h)], down_sem.at[t, h], m_recv.at[at, h], ctx=me - SIDES)

    def side_copy(at, ref, h):
        src = at * SIDES + b
        to = a * SIDES + 1 - b
        return send(ref.at[cut(h)], mall.at[src, cut(h)], side_sem.at[at, h], m_recv.at[src, h], ctx=to)

    def m_arrived(src, h):
        ref = mall.at[src, cut(h)]
        send(ref, ref, up_sem.at[0, 0], m_recv.at[src, h], ctx=a * SIDES + 1 - b).wait_recv()

    def mirror_copy():
        return send(
            w_hbm.at[q_own], fall.at[here, q_own], mirror_sem.at[0], f_recv.at[here, q_own], ctx=mirror
        )

    def fup_copy(t):
        at = (row - t) * SIDES + b
        ref = fall.at[at, q_own]
        return send(ref, ref, fup_sem.at[t], f_recv.at[at, q_own], ctx=me + SIDES)

    def fdown_copy(t):
        at = (row + t) * SIDES + b
        ref = fall.at[at, q_own]
        return send(ref, ref, fdown_sem.at[t], f_recv.at[at, q_own], ctx=me - SIDES)

    def fside_copy(at):
        src = at * SIDES + b
        ref = fall.at[src, q_own]
        return send(ref, ref, fside_sem.at[at], f_recv.at[src, q_own], ctx=a * SIDES + 1 - b)

    def fx_copy(src):
        ref = fall.at[src, q_own]
        return send(ref, ref, fx_sem.at[src], f_recv.at[src, q_own], dp=q_far)

    def fcore_copy(src, which):
        at = (q_own, q_far)[which]
        ref = fall.at[src, at]
        return send(ref, ref, fcore_sem.at[src, which], f_recv.at[src, at], dp=partner)

    def f_arrived(src, at):
        ref = fall.at[src, at]
        send(ref, ref, fup_sem.at[0], f_recv.at[src, at], ctx=a * SIDES + 1 - b).wait_recv()

    def core_copy(x):
        return send(
            part.at[2 * x + 1 - core], core_got.at[x], c_send.at[x], c_recv.at[x], dp=partner
        )

    def x_copy(r):
        peer = (rep + 2 * r) % replicas
        return send(x_out.at[r - 1], x_got.at[r - 1], x_send.at[r - 1], x_recv.at[r - 1], dp=peer)

    def when(condition, body):
        pl.when(condition)(body)

    for r in range(1, n):
        owner_copy(r).start()
    for h in range(CUTS):
        when(a + 1 < line, lambda h=h: up_copy(0, m_hbm, h).start())
        when(a > 0, lambda h=h: down_copy(0, m_hbm, h).start())
        side_copy(a, m_hbm, h).start()
    mirror_copy().start()

    locals_[0].wait()

    def turn(j, carry):
        over = pl.ds(pl.multiple_of(j * LANES, LANES), LANES)
        pre_send[over, :] = jnp.transpose(pre[:, over].astype(F32)).astype(BF16)
        return carry

    lax.fori_loop(0, units // LANES, turn, 0)
    own_pre = pltpu.make_async_copy(unit_rows(me), pre_place(), local_sem.at[8])
    own_pre.start()
    rope_tables(pos_ref, c_ref, s_ref)
    full[...] = jnp.zeros_like(full)
    slotted[...] = jnp.zeros_like(slotted)
    for copy in locals_[1:5]:
        copy.wait()

    def both(t, at, count, body):
        if t == 0:
            body(at, None)
        else:
            when(at - t >= 0, lambda: body(at - t, True))
            when(at + t < count, lambda: body(at + t, False))

    def send_pre():
        for r in range(1, n):
            pre_copy(r).start()

    def token_event(t):
        def body(at, below):
            src = at * SIDES + b
            ref = mall.at[src]
            for h in range(CUTS):
                m_arrived(src, h)
                if below:
                    when(a + 1 < line, lambda h=h: up_copy(t, ref, h).start())
                else:
                    when(a > 0, lambda h=h: down_copy(t, ref, h).start())
                side_copy(at, ref, h).start()

        when((side == 1) & (a + t < line), lambda: body(a + t, False))
        when(a - t >= 0, lambda: body(a - t, True))
        when((side == 0) & (a + t < line), lambda: body(a + t, False))

    def across(src):
        if shared:
            fx_copy(src).start()
            fcore_copy(src, 0).start()

    def weight_event(t):
        def body(at, below):
            src = at * SIDES + b
            f_arrived(src, q_own)
            if below is not False:
                when(row + 1 < near_line, lambda: fup_copy(t).start())
            if below is not True:
                when(row > 0, lambda: fdown_copy(t).start())
            across(src)

        both(t, row, near_line, body)

    def weight_turn(t):
        both(t, row, near_line, lambda at, below: fside_copy(at).start())

    def weight_side_event(t):
        def body(at, below):
            src = at * SIDES + 1 - b
            f_arrived(src, q_own)
            across(src)

        both(t, row, near_line, body)

    def weight_far_event(t, other):
        def body(at, below):
            src = at * SIDES + (1 - b if other else b)
            if shared:
                f_arrived(src, q_far)
                fcore_copy(src, 1).start()

        both(t, row, near_line, body)

    def event(kind, *given):
        return functools.partial(kind, *given)

    order = [
        (1, event(token_event, 1)),
        (2, event(weight_event, 0)),
        (2, event(weight_turn, 0)),
        (3, event(token_event, 2)),
        (3, send_pre),
        (5, event(weight_side_event, 0)),
        (6, event(weight_event, 1)),
        (6, event(weight_turn, 1)),
        (6, event(weight_far_event, 0, False)),
    ]

    halves = 2
    span = features // halves
    steps = patches // WIN * halves

    def attend(i, carry):
        at = pl.ds(pl.multiple_of(i // halves * WIN, WIN), WIN)
        over = pl.ds(pl.multiple_of(i % halves * span, LANES), span)
        attention_part(
            at, over, (q_ref, k_ref, v_ref, g_ref), c_ref, s_ref, (dq_ref, dk_ref, dv_ref)
        )
        for step in range(steps):
            todo = [run for index, run in order if index == step]
            if todo:
                when(i == step, lambda todo=todo: [run() for run in todo] and None)
        return carry

    lax.fori_loop(0, steps, attend, 0)
    far = (1 - side) * (units // 2)

    def incline(j, carry):
        x = pre[:, pl.ds(pl.multiple_of(far + j * LANES, LANES), LANES)].astype(F32)
        cdf = 0.5 * (1.0 + lax.erf(x * 0.5**0.5))
        slope[:, pl.ds(pl.multiple_of(j * LANES, LANES), LANES)] = cdf + x * jnp.exp(-0.5 * x * x) * (
            2.0 * math.pi
        ) ** (-0.5)
        return carry

    lax.fori_loop(0, units // 2 // LANES, incline, 0)

    for copy in locals_[5:]:
        copy.wait()
    for r in range(1, n):
        owner_copy(r).wait()
    padded = -(-n // 16) * 16
    earlier = lax.broadcasted_iota(jnp.int32, (rows_here, rows_here), 0) < lax.broadcasted_iota(
        jnp.int32, (rows_here, rows_here), 1
    )
    earlier = earlier.astype(F32).astype(BF16)
    names = lax.broadcasted_iota(jnp.int32, (padded, rows_here), 0)
    base = jnp.zeros((padded, 1), F32)
    cap = slots // n
    mine_only = lax.broadcasted_iota(jnp.int32, (padded, 1), 0) == me
    lane_of = lax.broadcasted_iota(jnp.int32, (1, slots), 1)
    in_source = (lane_of % cap).astype(F32)
    slot_of = jnp.full((1, slots), -1.0, F32)
    for s in range(n):
        onehot = (names == owners[s]).astype(F32)
        count = dot(onehot.astype(BF16), earlier)
        named = names.astype(F32)
        position = jnp.sum(onehot * (count + base + named * float(slots)), axis=0, keepdims=True)
        ranked = jnp.sum(onehot * (count + named * float(slots // 2)), axis=0, keepdims=True)
        tally = jnp.sum(onehot, axis=1, keepdims=True)
        start = jnp.sum(jnp.where(mine_only, base, 0.0), axis=0, keepdims=True)
        held = jnp.sum(jnp.where(mine_only, tally, 0.0), axis=0, keepdims=True)
        spot_of = jnp.where(in_source < held, start + in_source, -1.0)
        slot_of = jnp.where(lane_of // cap == s, spot_of, slot_of)
        base = base + tally
        lo = s % SIDES * rows_here
        code[s // SIDES, :, lo : lo + rows_here] = jnp.broadcast_to(position, (8, rows_here))
        ranks[s // SIDES, :, lo : lo + rows_here] = jnp.broadcast_to(
            ranked + float(s % near * cap), (8, rows_here)
        )
    standing = lax.broadcasted_iota(jnp.int32, (slots, block), 0).astype(F32)

    def landing(o, t):
        first = (o * slots).astype(F32)
        return (standing == code[t, 0:1, :] - first).astype(F32).astype(BF16)

    def nth(d):
        low = jnp.where(d <= a, a - d, d)
        flip = line - 1 - a
        high = line - 1 - jnp.where(d <= flip, flip - d, d)
        return jnp.where(side == 0, low, high)

    def gathered(t):
        return jnp.concatenate([mall[t * SIDES + i] for i in range(SIDES)], axis=0)

    def slotting(t, rows):
        slotted[...] += dot(landing(me, t), rows).astype(BF16)

    def early(d, carry):
        t = nth(d)
        for h in range(CUTS):
            m_arrived(t * SIDES + 1 - b, h)
        rows = gathered(t)
        linear_ref[t] = dot(w_ref[...].reshape(mine, width), rows, NT)
        slotting(t, rows)
        return carry

    def activation(t):
        spots = jnp.concatenate([landing(jnp.int32(o), t) for o in range(n)], axis=0)
        x = dot(pre_got[...], spots)
        cdf = 0.5 * (1.0 + lax.erf(x * 0.5**0.5))
        incline = cdf + x * jnp.exp(-0.5 * x * x) * (2.0 * math.pi) ** (-0.5)
        return (x * cdf).astype(BF16), incline

    ranking = lax.broadcasted_iota(jnp.int32, (slots // 2, block), 0).astype(F32)

    def send_hidden(phase):
        first = turn_side(phase) * near_line
        lanes = half_lanes(phase)
        blocks = pl.ds(pl.multiple_of(first * block, LANES), near_line * block)

        def outgoing(i, carry):
            shift = ((side * near + i) * (slots // 2)).astype(F32)
            spots = [ranking == ranks[first + j, 0:1, :] - shift for j in range(near_line)]
            spots = jnp.concatenate([spot.astype(F32).astype(BF16) for spot in spots], axis=1)
            hid_out[i, :, lanes] = dot(hid[:, blocks], spots, NT).astype(BF16)
            return carry

        lax.fori_loop(0, near, outgoing, 0)
        for r in range(1, near):
            hidden_copy(r, phase).start()
        own_hidden(phase).start()

    def own_hidden(phase):
        lanes = half_lanes(phase)
        return pltpu.make_async_copy(
            hid_out.at[here, :, lanes], hid_got.at[here, :, lanes], local_sem.at[9 + phase]
        )

    def hid_place(t):
        return pl.ds(pl.multiple_of(t * block, LANES), block)

    def late(d, carry):
        t = nth(d)
        act, incline = activation(t)
        hid[:, hid_place(t)] = (linear_ref[t] * incline).astype(BF16)
        full[...] += dot(act, gathered(t))
        return carry

    lax.fori_loop(0, line - 1, early, 0)
    for t in range(2, near_line):
        weight_event(t)
        weight_turn(t)
    weight_far_event(0, True)
    for t in range(1, near_line):
        weight_far_event(t, False)
    for t in range(3, line):
        token_event(t)
    for r in range(1, n):
        pre_copy(r).wait()
    own_pre.wait()
    lax.fori_loop(0, near_line, late, 0)
    for t in range(1, near_line):
        weight_side_event(t)
    send_hidden(0)
    lax.fori_loop(near_line, line - 1, late, 0)
    last = nth(jnp.int32(line - 1))
    act_ref[...], linear_ref[last] = activation(last)
    for h in range(CUTS):
        m_arrived(last * SIDES + 1 - b, h)
    full[...] += dot(act_ref[...], gathered(last))


    piece = width // replicas
    span_out = part.shape[2]
    for d in range(replicas):
        lo = d * piece // LANES * LANES
        hi = -(-(d + 1) * piece // LANES) * LANES
        shift = d * piece - lo
        value = full[:, lo:hi]
        if shift:
            value = pltpu.roll(value, hi - lo - shift, 1)
        part[d] = value[:, :span_out]
    for r in range(1, chips + 1):
        core_copy((place + r) % chips).start()
    late_rows = gathered(last)
    late_linear = dot(w_ref[...].reshape(mine, width), late_rows, NT)
    hid[:, hid_place(last)] = (late_linear * linear_ref[last]).astype(BF16)
    send_hidden(1)

    tight = x_out.shape[1] < mine
    rest = piece % LANES
    whole = piece - rest
    lane = lax.broadcasted_iota(jnp.int32, (mine // 2, LANES), 1)

    def packed(value):
        if not tight:
            return value
        top, low = value[: mine // 2], value[mine // 2 :]
        low = pltpu.roll(low, rest, 1)
        seam = jnp.where(lane < rest, top[:, whole:], low[:, :LANES])
        return jnp.concatenate([top[:, :whole], seam, low[:, LANES:]], axis=1)

    def unpacked(value):
        if not tight:
            return value
        low = pltpu.roll(value[:, whole:], span_out - rest, 1)
        return jnp.concatenate([value[:, :span_out], low], axis=0)

    for r in range(1, chips):
        x = (place + r) % chips
        core_copy(x).wait()
        x_out[r - 1] = packed(part[2 * x + core] + core_got[x]).astype(x_out.dtype)
        x_copy(r).start()


    groups = next(g for g in range(near_line, 0, -1) if near_line % g == 0 and units // 2 // g % LANES == 0)
    run, each = near // groups, units // 2 // groups

    def linear(g, carry):
        if shared:

            def await_rest(i, carry):
                for other in (partner, (partner + 2) % replicas):
                    f_arrived(g * run + i, other)
                return carry

            lax.fori_loop(0, run, await_rest, 0)
        weight = fall[pl.ds(g * run, run)].reshape(each, width)
        over = pl.ds(pl.multiple_of(g * each, LANES), each)
        to = pl.ds(pl.multiple_of(far + g * each, LANES), each)
        h_ref[:, to] = (dot(slotted[...], weight, NT) * slope[:, over]).astype(BF16)
        return carry

    slotting(last, gathered(last))
    for t in range(1, near_line):
        weight_far_event(t, True)
    lax.fori_loop(0, groups, linear, 0)

    for phase in range(2):
        own_hidden(phase).wait()
        for r in range(1, near):
            hidden_copy(r, phase).wait()
    spot = lax.broadcasted_iota(jnp.int32, (slots, slots), 0).astype(F32) == slot_of
    spot = spot.astype(F32).astype(BF16)

    def settle(g, carry):
        rows = hid_got[pl.ds(g * run, run)].reshape(each, slots)
        to = pl.ds(pl.multiple_of(side * (units // 2) + g * each, LANES), each)
        h_ref[:, to] = dot(spot, rows, NT).astype(BF16)
        return carry

    lax.fori_loop(0, groups, settle, 0)

    core_copy(place).wait()
    total = part[rep] + core_got[place]
    for r in range(1, chips):
        x_copy(r).wait()
        total = total + unpacked(x_got[r - 1].astype(F32))
    wg_ref[...] = total[:, :piece] * (rows_here * n * replicas) ** (-0.5)

    def sent(t, carry):
        for h in range(CUTS):

            @pl.when((a - t >= 0) & (a + 1 < line))
            def _():
                up_copy(t, mall.at[me], h).wait_send()

            @pl.when((a + t < line) & (a > 0))
            def _():
                down_copy(t, mall.at[me], h).wait_send()

            side_copy(t, mall.at[me], h).wait_send()
        return carry

    lax.fori_loop(0, line, sent, 0)
    mirror_copy().wait_send()

    def weight_sent(t, carry):
        @pl.when((row - t >= 0) & (row + 1 < near_line))
        def _():
            fup_copy(t).wait_send()

        @pl.when((row + t < near_line) & (row > 0))
        def _():
            fdown_copy(t).wait_send()

        fside_copy(t).wait_send()
        return carry

    lax.fori_loop(0, near_line, weight_sent, 0)
    if shared:

        def passed(src, carry):
            fx_copy(src).wait_send()
            fcore_copy(src, 0).wait_send()
            fcore_copy(src, 1).wait_send()
            return carry

        lax.fori_loop(0, near, passed, 0)


def finish_kernel(*refs):
    count = len(refs) // 2
    copies = [pltpu.make_async_copy(refs[i], refs[count + i], refs[-1].at[i]) for i in range(count)]
    for copy in copies:
        copy.start()
    for copy in copies:
        copy.wait()


def fused(merged_grad, merged_owner, merger_pre, fc2_weight, query, key_states, value_states, out_grad, position):
    rows_here, width = merged_grad.shape
    n, replicas = lax.axis_size("ctx"), lax.axis_size("dp")
    slots, units = merger_pre.shape
    mine = units // n
    line = n // SIDES
    near = n // 2
    near_line = line // 2
    block = SIDES * rows_here
    piece = width // replicas
    chips = replicas // 2
    span_out = -(-piece // LANES) * LANES
    tight = piece % LANES * 2 == LANES and mine % 32 == 0
    across = (mine // 2, 2 * piece) if tight else (mine, span_out)
    parts = replicas if chips == 2 and mine % (16 * replicas) == 0 else 1
    vmem = pl.BlockSpec(memory_space=pltpu.VMEM)
    hbm = pl.BlockSpec(memory_space=pl.ANY)
    dma = pltpu.SemaphoreType.DMA
    like = jax.ShapeDtypeStruct(query.shape, BF16)
    shapes = [
        jax.ShapeDtypeStruct((slots, units), BF16),
        jax.ShapeDtypeStruct((mine, piece), F32),
        like,
        like,
        like,
    ]
    results = pl.pallas_call(
        functools.partial(fused_kernel, n, replicas),
        in_specs=[hbm, vmem] + [hbm] * 6 + [vmem],
        out_specs=[vmem] * 5,
        out_shape=[pltpu.VMEM(shape.shape, shape.dtype) for shape in shapes],
        scratch_shapes=[
            pltpu.VMEM((n, rows_here, width), BF16),
            pltpu.VMEM((n, 1, rows_here), jnp.int32),
            pltpu.VMEM((slots, units), BF16),
            pltpu.VMEM((slots, units // 2), F32),
            pltpu.VMEM((units, slots), BF16),
            pltpu.VMEM((mine, n * slots), BF16),
            pltpu.VMEM((near, parts, mine // parts, width), BF16),
            pltpu.VMEM((parts, mine // parts, width), BF16),
            pltpu.VMEM((line, 8, block), F32),
            pltpu.VMEM((line, 8, block), F32),
            pltpu.VMEM((slots, width), BF16),
            pltpu.VMEM((mine, line * block), BF16),
            pltpu.VMEM((line, mine, block), F32),
            pltpu.VMEM((mine, block), BF16),
            pltpu.VMEM((near, mine, slots), BF16),
            pltpu.VMEM((near, mine, slots), BF16),
            pltpu.VMEM((mine, width), F32),
            pltpu.VMEM((replicas, mine, span_out), F32),
            pltpu.VMEM((chips, mine, span_out), F32),
            pltpu.VMEM((max(chips - 1, 1), *across), BF16),
            pltpu.VMEM((max(chips - 1, 1), *across), BF16),
        ]
        + [pltpu.VMEM(query.shape, BF16)] * 4
        + [
            pltpu.VMEM((query.shape[0], LANES), F32),
            pltpu.VMEM((query.shape[0], LANES), F32),
            dma((n, CUTS)),
            dma((line, CUTS)),
            dma((line, CUTS)),
            dma((line, CUTS)),
            dma((n - 1,)),
            dma((n - 1,)),
            dma((n - 1,)),
            dma((n - 1,)),
            dma((near, parts)),
            dma((1,)),
            dma((near_line,)),
            dma((near_line,)),
            dma((near_line,)),
            dma((near,)),
            dma((near, 2)),
            dma((near - 1, 2)),
            dma((near - 1, 2)),
            dma((chips,)),
            dma((chips,)),
            dma((max(chips - 1, 1),)),
            dma((max(chips - 1, 1),)),
            dma((11,)),
        ],
        compiler_params=pltpu.CompilerParams(
            collective_id=0, has_side_effects=True, vmem_limit_bytes=60 * 2**20
        ),
        name="fused",
    )(
        merged_grad,
        merged_owner.reshape(1, rows_here),
        merger_pre,
        fc2_weight.reshape(parts, mine // parts, width),
        query,
        key_states,
        value_states,
        out_grad,
        position,
    )
    return tuple(
        pl.pallas_call(
            finish_kernel,
            in_specs=[vmem] * 5,
            out_specs=[hbm] * 5,
            out_shape=shapes,
            scratch_shapes=[dma((5,))],
            compiler_params=pltpu.CompilerParams(vmem_limit_bytes=2**20),
            name="finish",
        )(*results)
    )


def solution(mesh):
    every = P(("dp", "ctx"), None)
    return jax.shard_map(
        fused,
        mesh=mesh,
        in_specs=(every, every, every, P("ctx", None)) + (every,) * 4 + (P(None, ("dp", "ctx")),),
        out_specs=(every, P("ctx", "dp")) + (every,) * 3,
        check_vma=False,
    )
```

```python
import functools
import math

import jax
import jax.numpy as jnp
from jax import lax
from jax.experimental import pallas as pl
from jax.experimental.pallas import tpu as pltpu
from jax.sharding import PartitionSpec as P

HEAD = 80
WIN = 64
LANES = 128
SIDES = 2
CUTS = 2
F32 = jnp.float32
BF16 = jnp.bfloat16
MESH = pl.DeviceIdType.MESH
NT = (((1,), (1,)), ((), ()))
TN = (((0,), (0,)), ((), ()))
NN = (((1,), (0,)), ((), ()))


def dot(a, b, dims=NN):
    return lax.dot_general(a, b, dims, preferred_element_type=F32)


def spread(table, width):
    shape = (LANES, width)
    lane = lax.broadcasted_iota(jnp.int32, shape, 1) % HEAD
    pick = (lane == lax.broadcasted_iota(jnp.int32, shape, 0)).astype(F32).astype(BF16)
    high = table.astype(BF16)
    rest = table - high.astype(F32)
    mid = rest.astype(BF16)
    low = (rest - mid.astype(F32)).astype(BF16)
    return dot(high, pick) + dot(mid, pick) + dot(low, pick)


def rope_tables(pos_ref, c_ref, s_ref):
    count = pos_ref.shape[1]
    half, quarter = HEAD // 2, HEAD // 4
    unit = lax.broadcasted_iota(jnp.int32, (LANES, count), 0)
    rows = pos_ref[0:1, :].astype(F32)
    cols = pos_ref[1:2, :].astype(F32)
    rank = (unit % half % quarter).astype(F32)
    freq = jnp.exp(rank * (-4.0 / HEAD * math.log(10000.0)))
    angles = jnp.where(unit % half < quarter, rows, cols) * freq
    c_ref[...] = jnp.transpose(jnp.cos(angles))
    s_ref[...] = jnp.transpose(jnp.where(unit < half, -1.0, 1.0) * jnp.sin(angles))


def attention_part(at, over, refs, c_ref, s_ref, outs):
    q_ref, k_ref, v_ref, g_ref = refs
    dq_ref, dk_ref, dv_ref = outs
    width = over.size
    heads = width // HEAD
    half = HEAD // 2
    cosine = spread(c_ref[at, :], width)
    sine = spread(s_ref[at, :], width)
    lane = lax.broadcasted_iota(jnp.int32, (WIN, width), 1)
    first = lane % HEAD < half

    def swap(x):
        return jnp.where(first, pltpu.roll(x, width - half, 1), pltpu.roll(x, half, 1))

    def rotated(x):
        return (x * cosine + swap(x) * sine).astype(BF16)

    def unrotated(x):
        return (x * cosine - swap(x) * sine).astype(BF16)

    q = rotated(q_ref[at, over].astype(F32))
    k = rotated(k_ref[at, over].astype(F32))
    v = v_ref[at, over]
    g = g_ref[at, over]
    factor = HEAD ** (-0.5)
    dq, dk, dv = {}, {}, {}

    def add(into, tile, value):
        for i in range(value.shape[1] // LANES):
            part = value[:, i * LANES : (i + 1) * LANES]
            into[tile + i] = into[tile + i] + part if tile + i in into else part

    for head in range(heads):
        tile = head * HEAD // LANES
        end = -(-(head + 1) * HEAD // LANES)
        lo, hi = tile * LANES, end * LANES
        here = lax.broadcasted_iota(jnp.int32, (1, hi - lo), 1) + lo
        mask = ((here >= head * HEAD) & (here < (head + 1) * HEAD)).astype(F32).astype(BF16)
        qm = q[:, lo:hi] * mask
        km = k[:, lo:hi] * mask
        gm = g[:, lo:hi] * mask
        scores = dot(qm, k[:, lo:hi], NT) * factor
        weight = jnp.exp(scores - jnp.max(scores, axis=1, keepdims=True))
        probs = weight * (1.0 / jnp.sum(weight, axis=1, keepdims=True))
        probs_b = probs.astype(BF16)
        prob_grad = dot(gm, v[:, lo:hi], NT)
        delta = jnp.sum(probs_b.astype(F32) * prob_grad, axis=1, keepdims=True)
        score_grad = (probs * (prob_grad - delta)).astype(BF16)
        add(dv, tile, dot(probs_b, gm, TN))
        add(dq, tile, dot(score_grad, km, NN))
        add(dk, tile, dot(score_grad, qm, TN))

    def joined(parts):
        return jnp.concatenate([parts[i] for i in range(width // LANES)], axis=1)

    dq_ref[at, over] = unrotated(joined(dq) * factor)
    dk_ref[at, over] = unrotated(joined(dk) * factor)
    dv_ref[at, over] = joined(dv).astype(BF16)


def fused_kernel(
    n,
    replicas,
    m_hbm,
    o_ref,
    p_hbm,
    w_hbm,
    q_hbm,
    k_hbm,
    v_hbm,
    g_hbm,
    pos_ref,
    h_ref,
    wg_ref,
    dq_ref,
    dk_ref,
    dv_ref,
    mall,
    owners,
    pre,
    slope,
    pre_send,
    pre_got,
    fall,
    w_ref,
    code,
    ranks,
    slotted,
    hid,
    linear_ref,
    act_ref,
    hid_out,
    hid_got,
    full,
    part,
    core_got,
    x_out,
    x_got,
    q_ref,
    k_ref,
    v_ref,
    g_ref,
    c_ref,
    s_ref,
    m_recv,
    up_sem,
    down_sem,
    side_sem,
    o_send,
    o_recv,
    p_send,
    p_recv,
    f_recv,
    mirror_sem,
    fup_sem,
    fdown_sem,
    fside_sem,
    fx_sem,
    fcore_sem,
    h_send,
    h_recv,
    c_send,
    c_recv,
    x_send,
    x_recv,
    local_sem,
):
    line = n // SIDES
    near = n // 2
    near_line = line // 2
    rows_here, width = m_hbm.shape
    slots, units = pre.shape
    mine = units // n
    parts = w_hbm.shape[0]
    shared = parts > 1
    block = SIDES * rows_here
    patches, features = q_ref.shape
    chips = replicas // 2
    me = lax.axis_index("ctx")
    rep = lax.axis_index("dp")
    a, b = me // SIDES, me % SIDES
    side, row = a // near_line, a % near_line
    here = me % near
    mirror = (me + near) % n
    partner = rep // 2 * 2 + 1 - rep % 2
    core, place = rep % 2, rep // 2
    q_own = rep if shared else 0
    q_far = (rep + 2) % replicas if shared else 0

    barrier = pltpu.get_barrier_semaphore()
    for r in range(1, n):
        pl.semaphore_signal(barrier, inc=1, device_id={"dp": rep, "ctx": (me + r) % n}, device_id_type=MESH)
    pl.semaphore_signal(barrier, inc=1, device_id={"dp": partner, "ctx": me}, device_id_type=MESH)
    for r in range(1, chips):
        pl.semaphore_signal(
            barrier, inc=1, device_id={"dp": (rep + 2 * r) % replicas, "ctx": me}, device_id_type=MESH
        )
    locals_ = [
        pltpu.make_async_copy(p_hbm, pre, local_sem.at[0]),
        pltpu.make_async_copy(q_hbm, q_ref, local_sem.at[1]),
        pltpu.make_async_copy(k_hbm, k_ref, local_sem.at[2]),
        pltpu.make_async_copy(v_hbm, v_ref, local_sem.at[3]),
        pltpu.make_async_copy(g_hbm, g_ref, local_sem.at[4]),
        pltpu.make_async_copy(m_hbm, mall.at[me], local_sem.at[5]),
        pltpu.make_async_copy(w_hbm, w_ref, local_sem.at[6]),
        pltpu.make_async_copy(o_ref, owners.at[me], local_sem.at[7]),
    ]
    for copy in locals_:
        copy.start()
    pl.semaphore_wait(barrier, n - 1 + chips)

    def send(src, dst, send_sem, recv_sem, ctx=None, dp=None):
        where = {"dp": rep if dp is None else dp, "ctx": me if ctx is None else ctx}
        return pltpu.make_async_remote_copy(
            src_ref=src,
            dst_ref=dst,
            send_sem=send_sem,
            recv_sem=recv_sem,
            device_id=where,
            device_id_type=MESH,
        )

    def owner_copy(r):
        return send(o_ref, owners.at[me], o_send.at[r - 1], o_recv.at[r - 1], ctx=(me + r) % n)

    def unit_rows(peer):
        return pre_send.at[pl.ds(pl.multiple_of(peer * mine, 16), mine), :]

    def pre_place():
        return pre_got.at[:, pl.ds(pl.multiple_of(me * slots, LANES), slots)]

    def pre_copy(r):
        peer = (me + r) % n
        return send(unit_rows(peer), pre_place(), p_send.at[r - 1], p_recv.at[r - 1], ctx=peer)

    def turn_side(phase):
        return side if phase == 0 else 1 - side

    def half_lanes(phase):
        return pl.ds(pl.multiple_of(turn_side(phase) * (slots // 2), LANES), slots // 2)

    def hidden_copy(r, phase):
        to = (here + r) % near
        lanes = half_lanes(phase)
        return send(
            hid_out.at[to, :, lanes],
            hid_got.at[here, :, lanes],
            h_send.at[r - 1, phase],
            h_recv.at[r - 1, phase],
            ctx=side * near + to,
        )

    def cut(h):
        return pl.ds(h * (rows_here // CUTS), rows_here // CUTS)

    def up_copy(t, ref, h):
        at = (a - t) * SIDES + b
        return send(ref.at[cut(h)], mall.at[at, cut(h)], up_sem.at[t, h], m_recv.at[at, h], ctx=me + SIDES)

    def down_copy(t, ref, h):
        at = (a + t) * SIDES + b
        return send(ref.at[cut(h)], mall.at[at, cut(h)], down_sem.at[t, h], m_recv.at[at, h], ctx=me - SIDES)

    def side_copy(at, ref, h):
        src = at * SIDES + b
        to = a * SIDES + 1 - b
        return send(ref.at[cut(h)], mall.at[src, cut(h)], side_sem.at[at, h], m_recv.at[src, h], ctx=to)

    def m_arrived(src, h):
        ref = mall.at[src, cut(h)]
        send(ref, ref, up_sem.at[0, 0], m_recv.at[src, h], ctx=a * SIDES + 1 - b).wait_recv()

    def mirror_copy():
        return send(
            w_hbm.at[q_own], fall.at[here, q_own], mirror_sem.at[0], f_recv.at[here, q_own], ctx=mirror
        )

    def fup_copy(t):
        at = (row - t) * SIDES + b
        ref = fall.at[at, q_own]
        return send(ref, ref, fup_sem.at[t], f_recv.at[at, q_own], ctx=me + SIDES)

    def fdown_copy(t):
        at = (row + t) * SIDES + b
        ref = fall.at[at, q_own]
        return send(ref, ref, fdown_sem.at[t], f_recv.at[at, q_own], ctx=me - SIDES)

    def fside_copy(at):
        src = at * SIDES + b
        ref = fall.at[src, q_own]
        return send(ref, ref, fside_sem.at[at], f_recv.at[src, q_own], ctx=a * SIDES + 1 - b)

    def fx_copy(src):
        ref = fall.at[src, q_own]
        return send(ref, ref, fx_sem.at[src], f_recv.at[src, q_own], dp=q_far)

    def fcore_copy(src, which):
        at = (q_own, q_far)[which]
        ref = fall.at[src, at]
        return send(ref, ref, fcore_sem.at[src, which], f_recv.at[src, at], dp=partner)

    def f_arrived(src, at):
        ref = fall.at[src, at]
        send(ref, ref, fup_sem.at[0], f_recv.at[src, at], ctx=a * SIDES + 1 - b).wait_recv()

    def core_copy(x):
        return send(
            part.at[2 * x + 1 - core], core_got.at[x], c_send.at[x], c_recv.at[x], dp=partner
        )

    def x_copy(r):
        peer = (rep + 2 * r) % replicas
        return send(x_out.at[r - 1], x_got.at[r - 1], x_send.at[r - 1], x_recv.at[r - 1], dp=peer)

    def when(condition, body):
        pl.when(condition)(body)

    for r in range(1, n):
        owner_copy(r).start()
    for h in range(CUTS):
        when(a + 1 < line, lambda h=h: up_copy(0, m_hbm, h).start())
        when(a > 0, lambda h=h: down_copy(0, m_hbm, h).start())
        side_copy(a, m_hbm, h).start()
    mirror_copy().start()

    locals_[0].wait()

    def turn(j, carry):
        over = pl.ds(pl.multiple_of(j * LANES, LANES), LANES)
        pre_send[over, :] = jnp.transpose(pre[:, over].astype(F32)).astype(BF16)
        return carry

    lax.fori_loop(0, units // LANES, turn, 0)
    own_pre = pltpu.make_async_copy(unit_rows(me), pre_place(), local_sem.at[8])
    own_pre.start()
    rope_tables(pos_ref, c_ref, s_ref)
    full[...] = jnp.zeros_like(full)
    slotted[...] = jnp.zeros_like(slotted)
    for copy in locals_[1:5]:
        copy.wait()

    def both(t, at, count, body):
        if t == 0:
            body(at, None)
        else:
            when(at - t >= 0, lambda: body(at - t, True))
            when(at + t < count, lambda: body(at + t, False))

    def send_pre():
        for r in range(1, n):
            pre_copy(r).start()

    def token_event(t):
        def body(at, below):
            src = at * SIDES + b
            ref = mall.at[src]
            for h in range(CUTS):
                m_arrived(src, h)
                if below:
                    when(a + 1 < line, lambda h=h: up_copy(t, ref, h).start())
                else:
                    when(a > 0, lambda h=h: down_copy(t, ref, h).start())
                side_copy(at, ref, h).start()

        when((side == 1) & (a + t < line), lambda: body(a + t, False))
        when(a - t >= 0, lambda: body(a - t, True))
        when((side == 0) & (a + t < line), lambda: body(a + t, False))

    def across(src):
        if shared:
            fx_copy(src).start()
            fcore_copy(src, 0).start()

    def weight_event(t):
        def body(at, below):
            src = at * SIDES + b
            f_arrived(src, q_own)
            if below is not False:
                when(row + 1 < near_line, lambda: fup_copy(t).start())
            if below is not True:
                when(row > 0, lambda: fdown_copy(t).start())
            across(src)

        both(t, row, near_line, body)

    def weight_turn(t):
        both(t, row, near_line, lambda at, below: fside_copy(at).start())

    def weight_side_event(t):
        def body(at, below):
            src = at * SIDES + 1 - b
            f_arrived(src, q_own)
            across(src)

        both(t, row, near_line, body)

    def weight_far_event(t, other):
        def body(at, below):
            src = at * SIDES + (1 - b if other else b)
            if shared:
                f_arrived(src, q_far)
                fcore_copy(src, 1).start()

        both(t, row, near_line, body)

    def event(kind, *given):
        return functools.partial(kind, *given)

    order = [
        (1, event(token_event, 1)),
        (2, event(weight_event, 0)),
        (2, event(weight_turn, 0)),
        (3, event(token_event, 2)),
        (3, send_pre),
        (4, event(weight_event, 1)),
        (4, event(weight_turn, 1)),
        (4, event(weight_side_event, 0)),
        (6, event(weight_far_event, 0, False)),
    ]

    halves = 2
    span = features // halves
    steps = patches // WIN * halves

    def attend(i, carry):
        at = pl.ds(pl.multiple_of(i // halves * WIN, WIN), WIN)
        over = pl.ds(pl.multiple_of(i % halves * span, LANES), span)
        attention_part(
            at, over, (q_ref, k_ref, v_ref, g_ref), c_ref, s_ref, (dq_ref, dk_ref, dv_ref)
        )
        for step in range(steps):
            todo = [run for index, run in order if index == step]
            if todo:
                when(i == step, lambda todo=todo: [run() for run in todo] and None)
        return carry

    lax.fori_loop(0, steps, attend, 0)
    far = (1 - side) * (units // 2)

    def incline(j, carry):
        x = pre[:, pl.ds(pl.multiple_of(far + j * LANES, LANES), LANES)].astype(F32)
        cdf = 0.5 * (1.0 + lax.erf(x * 0.5**0.5))
        slope[:, pl.ds(pl.multiple_of(j * LANES, LANES), LANES)] = cdf + x * jnp.exp(-0.5 * x * x) * (
            2.0 * math.pi
        ) ** (-0.5)
        return carry

    lax.fori_loop(0, units // 2 // LANES, incline, 0)

    for copy in locals_[5:]:
        copy.wait()
    for r in range(1, n):
        owner_copy(r).wait()
    padded = -(-n // 16) * 16
    earlier = lax.broadcasted_iota(jnp.int32, (rows_here, rows_here), 0) < lax.broadcasted_iota(
        jnp.int32, (rows_here, rows_here), 1
    )
    earlier = earlier.astype(F32).astype(BF16)
    names = lax.broadcasted_iota(jnp.int32, (padded, rows_here), 0)
    base = jnp.zeros((padded, 1), F32)
    cap = slots // n
    mine_only = lax.broadcasted_iota(jnp.int32, (padded, 1), 0) == me
    lane_of = lax.broadcasted_iota(jnp.int32, (1, slots), 1)
    in_source = (lane_of % cap).astype(F32)
    slot_of = jnp.full((1, slots), -1.0, F32)
    for s in range(n):
        onehot = (names == owners[s]).astype(F32)
        count = dot(onehot.astype(BF16), earlier)
        named = names.astype(F32)
        position = jnp.sum(onehot * (count + base + named * float(slots)), axis=0, keepdims=True)
        ranked = jnp.sum(onehot * (count + named * float(slots // 2)), axis=0, keepdims=True)
        tally = jnp.sum(onehot, axis=1, keepdims=True)
        start = jnp.sum(jnp.where(mine_only, base, 0.0), axis=0, keepdims=True)
        held = jnp.sum(jnp.where(mine_only, tally, 0.0), axis=0, keepdims=True)
        spot_of = jnp.where(in_source < held, start + in_source, -1.0)
        slot_of = jnp.where(lane_of // cap == s, spot_of, slot_of)
        base = base + tally
        lo = s % SIDES * rows_here
        code[s // SIDES, :, lo : lo + rows_here] = jnp.broadcast_to(position, (8, rows_here))
        ranks[s // SIDES, :, lo : lo + rows_here] = jnp.broadcast_to(
            ranked + float(s % near * cap), (8, rows_here)
        )
    standing = lax.broadcasted_iota(jnp.int32, (slots, block), 0).astype(F32)

    def landing(o, t):
        first = (o * slots).astype(F32)
        return (standing == code[t, 0:1, :] - first).astype(F32).astype(BF16)

    def nth(d):
        low = jnp.where(d <= a, a - d, d)
        flip = line - 1 - a
        high = line - 1 - jnp.where(d <= flip, flip - d, d)
        return jnp.where(side == 0, low, high)

    def gathered(t):
        return jnp.concatenate([mall[t * SIDES + i] for i in range(SIDES)], axis=0)

    def slotting(t, rows):
        slotted[...] += dot(landing(me, t), rows).astype(BF16)

    def early(d, carry):
        t = nth(d)
        for h in range(CUTS):
            m_arrived(t * SIDES + 1 - b, h)
        rows = gathered(t)
        linear_ref[t] = dot(w_ref[...].reshape(mine, width), rows, NT)
        slotting(t, rows)
        return carry

    def activation(t):
        spots = jnp.concatenate([landing(jnp.int32(o), t) for o in range(n)], axis=0)
        x = dot(pre_got[...], spots)
        cdf = 0.5 * (1.0 + lax.erf(x * 0.5**0.5))
        incline = cdf + x * jnp.exp(-0.5 * x * x) * (2.0 * math.pi) ** (-0.5)
        return (x * cdf).astype(BF16), incline

    ranking = lax.broadcasted_iota(jnp.int32, (slots // 2, block), 0).astype(F32)

    def send_hidden(phase):
        first = turn_side(phase) * near_line
        lanes = half_lanes(phase)
        blocks = pl.ds(pl.multiple_of(first * block, LANES), near_line * block)

        def outgoing(i, carry):
            shift = ((side * near + i) * (slots // 2)).astype(F32)
            spots = [ranking == ranks[first + j, 0:1, :] - shift for j in range(near_line)]
            spots = jnp.concatenate([spot.astype(F32).astype(BF16) for spot in spots], axis=1)
            hid_out[i, :, lanes] = dot(hid[:, blocks], spots, NT).astype(BF16)
            return carry

        lax.fori_loop(0, near, outgoing, 0)
        for r in range(1, near):
            hidden_copy(r, phase).start()
        own_hidden(phase).start()

    def own_hidden(phase):
        lanes = half_lanes(phase)
        return pltpu.make_async_copy(
            hid_out.at[here, :, lanes], hid_got.at[here, :, lanes], local_sem.at[9 + phase]
        )

    def hid_place(t):
        return pl.ds(pl.multiple_of(t * block, LANES), block)

    def late(d, carry):
        t = nth(d)
        act, incline = activation(t)
        hid[:, hid_place(t)] = (linear_ref[t] * incline).astype(BF16)
        full[...] += dot(act, gathered(t))
        return carry

    lax.fori_loop(0, line - 1, early, 0)
    for t in range(2, near_line):
        weight_event(t)
        weight_turn(t)
    weight_far_event(0, True)
    for t in range(1, near_line):
        weight_far_event(t, False)
    for t in range(3, line):
        token_event(t)
    for r in range(1, n):
        pre_copy(r).wait()
    own_pre.wait()
    lax.fori_loop(0, near_line, late, 0)
    for t in range(1, near_line):
        weight_side_event(t)
    send_hidden(0)
    lax.fori_loop(near_line, line - 1, late, 0)
    last = nth(jnp.int32(line - 1))
    act_ref[...], linear_ref[last] = activation(last)
    for h in range(CUTS):
        m_arrived(last * SIDES + 1 - b, h)
    full[...] += dot(act_ref[...], gathered(last))


    piece = width // replicas
    span_out = part.shape[2]
    for d in range(replicas):
        lo = d * piece // LANES * LANES
        hi = -(-(d + 1) * piece // LANES) * LANES
        shift = d * piece - lo
        value = full[:, lo:hi]
        if shift:
            value = pltpu.roll(value, hi - lo - shift, 1)
        part[d] = value[:, :span_out]
    for r in range(1, chips + 1):
        core_copy((place + r) % chips).start()
    late_rows = gathered(last)
    late_linear = dot(w_ref[...].reshape(mine, width), late_rows, NT)
    hid[:, hid_place(last)] = (late_linear * linear_ref[last]).astype(BF16)
    send_hidden(1)

    tight = x_out.shape[1] < mine
    rest = piece % LANES
    whole = piece - rest
    lane = lax.broadcasted_iota(jnp.int32, (mine // 2, LANES), 1)

    def packed(value):
        if not tight:
            return value
        top, low = value[: mine // 2], value[mine // 2 :]
        low = pltpu.roll(low, rest, 1)
        seam = jnp.where(lane < rest, top[:, whole:], low[:, :LANES])
        return jnp.concatenate([top[:, :whole], seam, low[:, LANES:]], axis=1)

    def unpacked(value):
        if not tight:
            return value
        low = pltpu.roll(value[:, whole:], span_out - rest, 1)
        return jnp.concatenate([value[:, :span_out], low], axis=0)

    for r in range(1, chips):
        x = (place + r) % chips
        core_copy(x).wait()
        x_out[r - 1] = packed(part[2 * x + core] + core_got[x]).astype(x_out.dtype)
        x_copy(r).start()


    groups = next(g for g in range(near_line, 0, -1) if near_line % g == 0 and units // 2 // g % LANES == 0)
    run, each = near // groups, units // 2 // groups

    def linear(g, carry):
        if shared:

            def await_rest(i, carry):
                for other in (partner, (partner + 2) % replicas):
                    f_arrived(g * run + i, other)
                return carry

            lax.fori_loop(0, run, await_rest, 0)
        weight = fall[pl.ds(g * run, run)].reshape(each, width)
        over = pl.ds(pl.multiple_of(g * each, LANES), each)
        to = pl.ds(pl.multiple_of(far + g * each, LANES), each)
        h_ref[:, to] = (dot(slotted[...], weight, NT) * slope[:, over]).astype(BF16)
        return carry

    slotting(last, gathered(last))
    for t in range(1, near_line):
        weight_far_event(t, True)
    lax.fori_loop(0, groups, linear, 0)

    for phase in range(2):
        own_hidden(phase).wait()
        for r in range(1, near):
            hidden_copy(r, phase).wait()
    spot = lax.broadcasted_iota(jnp.int32, (slots, slots), 0).astype(F32) == slot_of
    spot = spot.astype(F32).astype(BF16)

    def settle(g, carry):
        rows = hid_got[pl.ds(g * run, run)].reshape(each, slots)
        to = pl.ds(pl.multiple_of(side * (units // 2) + g * each, LANES), each)
        h_ref[:, to] = dot(spot, rows, NT).astype(BF16)
        return carry

    lax.fori_loop(0, groups, settle, 0)

    core_copy(place).wait()
    total = part[rep] + core_got[place]
    for r in range(1, chips):
        x_copy(r).wait()
        total = total + unpacked(x_got[r - 1].astype(F32))
    wg_ref[...] = total[:, :piece] * (rows_here * n * replicas) ** (-0.5)

    def sent(t, carry):
        for h in range(CUTS):

            @pl.when((a - t >= 0) & (a + 1 < line))
            def _():
                up_copy(t, mall.at[me], h).wait_send()

            @pl.when((a + t < line) & (a > 0))
            def _():
                down_copy(t, mall.at[me], h).wait_send()

            side_copy(t, mall.at[me], h).wait_send()
        return carry

    lax.fori_loop(0, line, sent, 0)
    mirror_copy().wait_send()

    def weight_sent(t, carry):
        @pl.when((row - t >= 0) & (row + 1 < near_line))
        def _():
            fup_copy(t).wait_send()

        @pl.when((row + t < near_line) & (row > 0))
        def _():
            fdown_copy(t).wait_send()

        fside_copy(t).wait_send()
        return carry

    lax.fori_loop(0, near_line, weight_sent, 0)
    if shared:

        def passed(src, carry):
            fx_copy(src).wait_send()
            fcore_copy(src, 0).wait_send()
            fcore_copy(src, 1).wait_send()
            return carry

        lax.fori_loop(0, near, passed, 0)


def finish_kernel(*refs):
    count = len(refs) // 2
    copies = [pltpu.make_async_copy(refs[i], refs[count + i], refs[-1].at[i]) for i in range(count)]
    for copy in copies:
        copy.start()
    for copy in copies:
        copy.wait()


def fused(merged_grad, merged_owner, merger_pre, fc2_weight, query, key_states, value_states, out_grad, position):
    rows_here, width = merged_grad.shape
    n, replicas = lax.axis_size("ctx"), lax.axis_size("dp")
    slots, units = merger_pre.shape
    mine = units // n
    line = n // SIDES
    near = n // 2
    near_line = line // 2
    block = SIDES * rows_here
    piece = width // replicas
    chips = replicas // 2
    span_out = -(-piece // LANES) * LANES
    tight = piece % LANES * 2 == LANES and mine % 32 == 0
    across = (mine // 2, 2 * piece) if tight else (mine, span_out)
    parts = replicas if chips == 2 and mine % (16 * replicas) == 0 else 1
    vmem = pl.BlockSpec(memory_space=pltpu.VMEM)
    hbm = pl.BlockSpec(memory_space=pl.ANY)
    dma = pltpu.SemaphoreType.DMA
    like = jax.ShapeDtypeStruct(query.shape, BF16)
    shapes = [
        jax.ShapeDtypeStruct((slots, units), BF16),
        jax.ShapeDtypeStruct((mine, piece), F32),
        like,
        like,
        like,
    ]
    results = pl.pallas_call(
        functools.partial(fused_kernel, n, replicas),
        in_specs=[hbm, vmem] + [hbm] * 6 + [vmem],
        out_specs=[vmem] * 5,
        out_shape=[pltpu.VMEM(shape.shape, shape.dtype) for shape in shapes],
        scratch_shapes=[
            pltpu.VMEM((n, rows_here, width), BF16),
            pltpu.VMEM((n, 1, rows_here), jnp.int32),
            pltpu.VMEM((slots, units), BF16),
            pltpu.VMEM((slots, units // 2), F32),
            pltpu.VMEM((units, slots), BF16),
            pltpu.VMEM((mine, n * slots), BF16),
            pltpu.VMEM((near, parts, mine // parts, width), BF16),
            pltpu.VMEM((parts, mine // parts, width), BF16),
            pltpu.VMEM((line, 8, block), F32),
            pltpu.VMEM((line, 8, block), F32),
            pltpu.VMEM((slots, width), BF16),
            pltpu.VMEM((mine, line * block), BF16),
            pltpu.VMEM((line, mine, block), F32),
            pltpu.VMEM((mine, block), BF16),
            pltpu.VMEM((near, mine, slots), BF16),
            pltpu.VMEM((near, mine, slots), BF16),
            pltpu.VMEM((mine, width), F32),
            pltpu.VMEM((replicas, mine, span_out), F32),
            pltpu.VMEM((chips, mine, span_out), F32),
            pltpu.VMEM((max(chips - 1, 1), *across), BF16),
            pltpu.VMEM((max(chips - 1, 1), *across), BF16),
        ]
        + [pltpu.VMEM(query.shape, BF16)] * 4
        + [
            pltpu.VMEM((query.shape[0], LANES), F32),
            pltpu.VMEM((query.shape[0], LANES), F32),
            dma((n, CUTS)),
            dma((line, CUTS)),
            dma((line, CUTS)),
            dma((line, CUTS)),
            dma((n - 1,)),
            dma((n - 1,)),
            dma((n - 1,)),
            dma((n - 1,)),
            dma((near, parts)),
            dma((1,)),
            dma((near_line,)),
            dma((near_line,)),
            dma((near_line,)),
            dma((near,)),
            dma((near, 2)),
            dma((near - 1, 2)),
            dma((near - 1, 2)),
            dma((chips,)),
            dma((chips,)),
            dma((max(chips - 1, 1),)),
            dma((max(chips - 1, 1),)),
            dma((11,)),
        ],
        compiler_params=pltpu.CompilerParams(
            collective_id=0, has_side_effects=True, vmem_limit_bytes=60 * 2**20
        ),
        name="fused",
    )(
        merged_grad,
        merged_owner.reshape(1, rows_here),
        merger_pre,
        fc2_weight.reshape(parts, mine // parts, width),
        query,
        key_states,
        value_states,
        out_grad,
        position,
    )
    return tuple(
        pl.pallas_call(
            finish_kernel,
            in_specs=[vmem] * 5,
            out_specs=[hbm] * 5,
            out_shape=shapes,
            scratch_shapes=[dma((5,))],
            compiler_params=pltpu.CompilerParams(vmem_limit_bytes=2**20),
            name="finish",
        )(*results)
    )


def solution(mesh):
    every = P(("dp", "ctx"), None)
    return jax.shard_map(
        fused,
        mesh=mesh,
        in_specs=(every, every, every, P("ctx", None)) + (every,) * 4 + (P(None, ("dp", "ctx")),),
        out_specs=(every, P("ctx", "dp")) + (every,) * 3,
        check_vma=False,
    )
```
